32 devices in a mesh: row: 8 (over y, x, core), col: 4 (over z).
Axes of the slice: x: 2, y: 2, z: 4, core: 2. Of those that a mesh axis runs over, the one named last changes fastest.
Arguments:
- features: bfloat16 [65536, 256], P(('row', 'col')), may hold values from -6 to 6
- w_self: bfloat16 [256, 256], replicated, may hold values from -0.375 to 0.375
- w_neigh: bfloat16 [256, 256], replicated, may hold values from -1.5 to 1.5
- bias: float32 [256], replicated, may hold values from -3 to 3
- hub_ids: int32 [6], replicated, may hold values from 0 to 7
- hub_adj: bfloat16 [32, 6, 2048, 256], P(('row', 'col')), may hold values from 0 to 2, as said below
- send_tile: int32 [32, 4, 2], P(('row', 'col')), may hold values from 0 to 15
- recv_count: int32 [32, 4], P(('row', 'col')), may hold values from 0 to 2, as said below
- recv_dst: int32 [32, 4, 2], P(('row', 'col')), may hold values from 0 to 15
- recv_adj: bfloat16 [32, 4, 2, 128, 128], P(('row', 'col')), may hold values from 0 to 2, as said below
- cotangent: bfloat16 [65536, 256], P(('row', 'col')), may hold values from -6 to 6
Outputs:
- output: bfloat16 [65536, 256], P(('row', 'col'))
- feature_grad: bfloat16 [65536, 256], P(('row', 'col'))
The draws below stay inside these ranges and needn't reach their ends.
Inputs may be any that keep to these rules, and one draw needn't show every extreme that they name: `recv_count`: every device uses all 2 slots from at least one device of its row group. `hub_adj`: nonnegative edge weights. `recv_adj`: nonnegative edge weights.
All inputs are finite; a program needn't handle non-finite values.
Results may differ from the reference program's by a relative error of at most 0.0055.
Values may be sent and summed in bfloat16 or wider, within the bound.
No kernel may reach another device: no remote copies, remote signals or barrier semaphores. Data moves between devices by JAX's collectives and lax.ppermute only.
A program may use at most 64 MiB of HBM per device.

```python
import math
import jax
import jax.numpy as jnp
import numpy as np
from jax import lax

D = 256
OUT = 256
NODE_DEV = 2048
TILE = 128
HUB = 256
SECTIONS = 6
CAP = 2
NODES = 65536
BLOCKS = 32
N_ROW = 8
N_COL = 4


def draw_hub_adj(key, part):
    shape = (N_ROW * N_COL, SECTIONS, NODE_DEV, HUB)
    first, second = jax.random.split(jax.random.fold_in(key, 11))
    present = jax.random.uniform(first, shape) < 4.0 / HUB
    values = jnp.exp(jax.random.uniform(second, shape, minval=math.log(0.25), maxval=math.log(2.0)))
    return jnp.where(present, values, 0.0).astype(jnp.bfloat16)


def draw_recv_adj(key, part):
    shape = (N_ROW * N_COL, N_COL, CAP, TILE, TILE)
    first, second = jax.random.split(jax.random.fold_in(key, 23))
    present = jax.random.uniform(first, shape) < 4.0 / TILE
    values = jnp.exp(jax.random.uniform(second, shape, minval=math.log(0.25), maxval=math.log(2.0)))
    return jnp.where(present, values, 0.0).astype(jnp.bfloat16)


def draw_recv_count(key, part):
    first, second = jax.random.split(jax.random.fold_in(key, 37))
    base = jax.random.randint(first, (N_ROW * N_COL, N_COL), 0, CAP + 1)
    full_source = jax.random.randint(second, (N_ROW * N_COL, 1), 0, N_COL)
    positions = jnp.arange(N_COL, dtype=jnp.int32)[None, :]
    return jnp.where(positions == full_source, CAP, base).astype(jnp.int32)


def plant(result, key, smallest, high):
    longest = result.shape.index(max(result.shape))
    spots = []
    for shift in (0, 1):
        where = [jax.random.randint(jax.random.fold_in(key, axis), (), 0, length) for axis, length in enumerate(result.shape)]
        where[longest] = (where[longest] + shift) % result.shape[longest]
        spots.append(tuple(where))
    return result.at[spots[0]].set(smallest).at[spots[1]].set(high)


def level_of(own_key, extent, cuts, smallest, high):
    loudness, own = 1.0, jax.random.fold_in(own_key, 6)
    for position, blocks in cuts:
        steps = jnp.exp(jax.random.uniform(jax.random.fold_in(own, position), (blocks,), jnp.float32, smallest / len(cuts), high / len(cuts)))
        loudness = loudness * jnp.repeat(steps, extent[position] // blocks).reshape([-1 if axis == position else 1 for axis in range(len(extent))])
    return loudness


def rank_table(number_of, lean):
    loads = [(1 << 20) // math.isqrt(standing ** lean) + 1 for standing in range(1, number_of + 1)]
    spread = 1 + sum(loads) // (1 << 30)
    return np.cumsum(np.array([max(1, weight // spread) for weight in loads]))


def ranked(own_key, dims, number_of, lean):
    table = rank_table(number_of, lean)
    ticket = jax.random.randint(jax.random.fold_in(own_key, 1), dims, 0, int(table[number_of - 1]))
    rank = jnp.searchsorted(jnp.asarray(table, jnp.int32), ticket, side="right")
    return jax.random.permutation(jax.random.fold_in(own_key, 2), number_of)[rank].astype(jnp.int32)


def gaussian(own_key, dims, scale, most, cuts=(), held_as=jnp.bfloat16):
    values = jax.random.normal(own_key, dims, jnp.float32) * scale
    if len(cuts) > 0:
        values = level_of(own_key, dims, cuts, -0.22, 0.18) * values
    return jnp.clip(values, min=-most, max=most).astype(held_as)


def setup_inputs(seed: int = 0) -> dict:
    streams_of = jax.random.split(jax.random.key(seed), 12)
    return {
        "features": gaussian(streams_of[0], (NODES, D), 1.0, 6.0, ((0, 32),)),
        "w_self": gaussian(streams_of[1], (D, OUT), D ** -0.5, 0.375),
        "w_neigh": gaussian(streams_of[2], (D, OUT), (D // 16) ** -0.5, 1.5),
        "bias": gaussian(streams_of[3], (OUT,), 0.5, 3.0, (), jnp.float32),
        "hub_ids": plant(ranked(streams_of[4], (SECTIONS,), N_ROW, 2), jax.random.fold_in(streams_of[4], 3), 0, N_ROW - 1).astype(jnp.int32),
        "hub_adj": draw_hub_adj(jax.random.fold_in(streams_of[11], 71), 0),
        "send_tile": plant(jax.random.randint(streams_of[6], (BLOCKS, N_COL, CAP), 0, NODE_DEV // TILE), jax.random.fold_in(streams_of[6], 1), 0, (NODE_DEV // TILE) - 1).astype(jnp.int32),
        "recv_count": draw_recv_count(jax.random.fold_in(streams_of[11], 71), 0),
        "recv_dst": plant(jax.random.randint(streams_of[8], (BLOCKS, N_COL, CAP), 0, NODE_DEV // TILE), jax.random.fold_in(streams_of[8], 1), 0, (NODE_DEV // TILE) - 1).astype(jnp.int32),
        "recv_adj": draw_recv_adj(jax.random.fold_in(streams_of[11], 71), 0),
        "cotangent": gaussian(streams_of[10], (NODES, OUT), 1.0, 6.0, ((0, 32),)),
    }


def device_pass(feats, hadj, blocks, recv, count, dst, adj, cot, w_self, w_neigh, bias):
    f32 = jnp.float32
    nodes = feats.shape[0]
    width = feats.shape[1]
    peers, slots, tile = adj.shape[0], adj.shape[1], adj.shape[2]
    total = peers * slots
    count_tiles = nodes // tile
    live = (jnp.arange(slots, dtype=jnp.int32)[None, :] < count[:, None]).astype(f32).reshape(total)
    select = (dst.reshape(total)[:, None] == jnp.arange(count_tiles, dtype=jnp.int32)[None, :]).astype(f32) * live[:, None]
    adjs = adj.reshape(total, tile, tile).astype(f32)
    rec = recv.reshape(total, tile, width).astype(f32)
    contrib = jnp.einsum('sij,sjd->sid', adjs, rec)
    tile_sum = jnp.einsum('sn,sid->nid', select, contrib, precision=lax.Precision.HIGHEST).reshape(nodes, width)
    hadj_f = hadj.astype(f32)
    hub_sum = jnp.einsum('snh,shd->nd', hadj_f, blocks.astype(f32))
    tile_deg = jnp.einsum('sn,si->ni', select, jnp.sum(adjs, axis=2), precision=lax.Precision.HIGHEST).reshape(nodes)
    deg = 1.0 + jnp.sum(hadj_f, axis=(0, 2)) + tile_deg
    agg = ((tile_sum + hub_sum) / deg[:, None]).astype(jnp.bfloat16)
    pre = jnp.dot(feats, w_self, preferred_element_type=f32) + jnp.dot(agg, w_neigh, preferred_element_type=f32) + bias
    sig = jax.nn.sigmoid(pre)
    out = (pre * sig).astype(jnp.bfloat16)
    grad = (cot.astype(f32) * sig * (1.0 + pre * (1.0 - sig))).astype(jnp.bfloat16)
    self_grad = jnp.dot(grad, w_self.T, preferred_element_type=f32)
    agg_grad = (jnp.dot(grad, w_neigh.T, preferred_element_type=f32) / deg[:, None]).astype(jnp.bfloat16)
    hub_grad = jnp.einsum('snh,nd->shd', hadj_f, agg_grad.astype(f32))
    rows = agg_grad.reshape(count_tiles, tile, width)[dst.reshape(total)]
    slot_grad = (jnp.einsum('sij,sid->sjd', adjs, rows.astype(f32)) * live[:, None, None]).astype(jnp.bfloat16)
    return out, self_grad, hub_grad, slot_grad.reshape(peers, slots, tile, width)


def reference(features, w_self, w_neigh, bias, hub_ids, hub_adj, send_tile, recv_count, recv_dst, recv_adj, cotangent):
    f32 = jnp.float32
    grid = features.reshape(N_ROW, N_COL, NODE_DEV, D)
    hubs = grid[hub_ids][:, :, :HUB]
    hub_cols = jnp.transpose(hubs, (1, 0, 2, 3))
    count_tiles = NODE_DEV // TILE
    cot_blocks = cotangent.reshape(N_ROW * N_COL, NODE_DEV, OUT)
    columns = jnp.arange(N_COL, dtype=jnp.int32)

    def one_row(carry, row):
        start = (row * N_COL).astype(jnp.int32)
        rows_x = lax.dynamic_index_in_dim(grid, row, 0, keepdims=False)

        def take(array):
            return lax.dynamic_slice_in_dim(array, start, N_COL, 0)

        hadj = take(hub_adj)
        stile = take(send_tile)
        rcount = take(recv_count)
        rdst = take(recv_dst)
        radj = take(recv_adj)
        cot_rows = take(cot_blocks)
        tiles = rows_x.reshape(N_COL, count_tiles, TILE, D)
        picked = jnp.transpose(stile, (1, 0, 2))
        received = tiles[columns[None, :, None], picked]
        out, self_grad, hub_grad, slot_grad = jax.vmap(
            device_pass, in_axes=(0, 0, 0, 0, 0, 0, 0, 0, None, None, None))(
            rows_x, hadj, hub_cols, received, rcount, rdst, radj, cot_rows, w_self, w_neigh, bias)
        select = (stile[..., None] == jnp.arange(count_tiles, dtype=jnp.int32)).astype(f32)
        returned = jnp.einsum('pckn,cpkid->pnid', select, slot_grad.astype(f32),
                              precision=lax.Precision.HIGHEST).reshape(N_COL, NODE_DEV, D)
        return carry + hub_grad, (out, self_grad + returned)

    start_carry = jnp.zeros((N_COL, SECTIONS, HUB, D), f32)
    hub_total, (outs, grads) = lax.scan(one_row, start_carry, jnp.arange(N_ROW, dtype=jnp.int32))
    for section in range(SECTIONS):
        grads = grads.at[hub_ids[section], :, :HUB].add(hub_total[:, section])
    return outs.reshape(NODES, OUT), grads.reshape(NODES, D).astype(jnp.bfloat16)
```

```python
import functools

import jax
import jax.numpy as jnp
from jax import lax
from jax.experimental import pallas as pl
from jax.experimental.pallas import tpu as pltpu
from jax.sharding import PartitionSpec as P

F32 = jnp.float32
BF16 = jnp.bfloat16


def whole(*shape):
    return pl.BlockSpec(shape, lambda *_: (0,) * len(shape))


def pick_kernel(pos, send, feats, *rest, tile):
    outs, sems = rest[:-1], rest[-1]
    col = pos[1]
    copies = []
    for d, out in enumerate(outs):
        for k in range(out.shape[0]):
            start = pl.multiple_of(send[(col ^ d) * out.shape[0] + k] * tile, tile)
            copies.append(pltpu.make_async_copy(feats.at[pl.ds(start, tile)], out.at[k], sems.at[d, k]))
            copies[-1].start()
    for copy in copies:
        copy.wait()


def hub_forward_kernel(which, adj, *rest):
    blocks, (raw, deg) = rest[:-2], rest[-2:]
    total = None
    lanes = None
    for s, block in enumerate(blocks):
        weights = adj[s]
        part = jnp.dot(weights, block[0], preferred_element_type=F32)
        total = part if total is None else total + part
        wide = weights.astype(F32)
        for c in range(0, wide.shape[1], 128):
            lanes = wide[:, c : c + 128] if lanes is None else lanes + wide[:, c : c + 128]
    raw[...] = total
    deg[...] = jnp.broadcast_to(1.0 + jnp.sum(lanes, axis=1, keepdims=True), deg.shape)


def middle_kernel(pos, count, dst, raw_in, deg_in, feats, cot, adj, w_self, w_neigh, bias, *rest, peers, slots, tile):
    inc = rest[:peers]
    out, grad, agg_grad = rest[peers : peers + 3]
    back = rest[peers + 3 : 2 * peers + 3]
    raw, deg, kept = rest[2 * peers + 3 :]
    step = pl.program_id(0)
    rows = raw.shape[0]
    per = rows // tile
    col = pos[1]
    raw[...] = raw_in[...]
    deg[...] = deg_in[...]
    for d in range(peers):
        for k in range(slots):
            p = col ^ d
            target = dst[p * slots + k] - step * per

            @pl.when((k < count[p]) & (target >= 0) & (target < per))
            def _(d=d, k=k, p=p, target=target):
                at = pl.ds(pl.multiple_of(target * tile, tile), tile)
                weights = adj[p, k]
                raw[at, :] += jnp.dot(weights, inc[d][k], preferred_element_type=F32)
                deg[at, :] += jnp.sum(weights.astype(F32), axis=1, keepdims=True)

    inverse = 1.0 / deg[...]
    inverse = jnp.concatenate([inverse] * (raw.shape[1] // inverse.shape[1]), axis=1)
    agg = (raw[...] * inverse).astype(BF16)
    pre = (
        jnp.dot(feats[...], w_self[...], preferred_element_type=F32)
        + jnp.dot(agg, w_neigh[...], preferred_element_type=F32)
        + bias[...]
    )
    sig = 0.5 * jnp.tanh(0.5 * pre) + 0.5
    out[...] = (pre * sig).astype(BF16)
    g = (cot[...].astype(F32) * sig * (1.0 + pre * (1.0 - sig))).astype(BF16)
    grad[...] = g
    contract = (((1,), (1,)), ((), ()))
    a = (lax.dot_general(g, w_neigh[...], contract, preferred_element_type=F32) * inverse).astype(BF16)
    agg_grad[...] = a
    kept[pl.ds(pl.multiple_of(step * rows, rows), rows), :] = a

    @pl.when(step == pl.num_programs(0) - 1)
    def _():
        for d in range(peers):
            for k in range(slots):
                p = col ^ d
                at = pl.ds(pl.multiple_of(dst[p * slots + k] * tile, tile), tile)
                part = lax.dot_general(
                    adj[p, k], kept[at, :], (((0,), (0,)), ((), ())), preferred_element_type=F32
                )
                live = jnp.where(k < count[p], 1.0, 0.0).astype(F32)
                back[d][k] = (part * live).astype(BF16)


def hub_backward_kernel(which, adj, agg_grad, grad, w_self, even, odd, self_grad, acc):
    step = pl.program_id(0)
    sections = adj.shape[0]

    @pl.when(step == 0)
    def _():
        acc[...] = jnp.zeros_like(acc)

    turned = agg_grad[...].T
    for s in range(sections):
        acc[s] += jnp.dot(turned, adj[s], preferred_element_type=F32)
    self_grad[...] = lax.dot_general(grad[...], w_self[...], (((1,), (1,)), ((), ())), preferred_element_type=F32)

    @pl.when(step == pl.num_programs(0) - 1)
    def _():
        for e in range(even.shape[0]):
            for ref, owner in ((even, 2 * e), (odd, 2 * e + 1)):
                total = jnp.zeros(acc.shape[1:], F32)
                for s in range(sections):
                    total = total + acc[s] * jnp.where(which[s] == owner, 1.0, 0.0).astype(F32)
                ref[e] = total.astype(BF16)


def pair_add_kernel(even, came, *outs):
    for e, out in enumerate(outs):
        out[...] = (even[e].astype(F32) + came[e].astype(F32)).astype(BF16)


def final_kernel(pos, send, self_grad, *rest, peers, slots, tile):
    back, hub, out, total = rest[:peers], rest[peers:-2], rest[-2], rest[-1]
    step = pl.program_id(0)
    rows = total.shape[0]
    per = rows // tile
    col = pos[1]
    total[...] = self_grad[...]
    for d in range(peers):
        for k in range(slots):
            target = send[(col ^ d) * slots + k] - step * per

            @pl.when((target >= 0) & (target < per))
            def _(d=d, k=k, target=target):
                at = pl.ds(pl.multiple_of(target * tile, tile), tile)
                total[at, :] += back[d][k].astype(F32)

    @pl.when(step == 0)
    def _():
        come = hub[0][...].astype(F32)
        for h in hub[1:]:
            come = come + h[...].astype(F32)
        total[0 : come.shape[1], :] += come.T

    out[...] = total[...].astype(BF16)


def shards(
    features, w_self, w_neigh, bias, hub_ids, hub_adj, send_tile, recv_count, recv_dst, recv_adj, cotangent, *, n_row, n_col
):
    nodes, width = features.shape
    sections, hub_rows = hub_ids.shape[0], hub_adj.shape[3]
    peers, slots, tile = recv_adj.shape[1], recv_adj.shape[2], recv_adj.shape[3]
    out_width = w_self.shape[1]
    row, col = lax.axis_index("row"), lax.axis_index("col")
    pos = jnp.stack([row, col]).astype(jnp.int32)
    which = hub_ids ^ row
    send, count, dst = send_tile.reshape(-1), recv_count.reshape(-1), recv_dst.reshape(-1)
    params = functools.partial(pltpu.CompilerParams, vmem_limit_bytes=48 * 1024 * 1024)

    def across(x, axis, size, d):
        return lax.ppermute(x, axis, [(i, i ^ d) for i in range(size)])

    order = sorted(range(1, n_col), key=lambda d: (d != n_col // 2, -d))
    pair = jax.ShapeDtypeStruct((slots, tile, width), BF16)
    picked = pl.pallas_call(
        functools.partial(pick_kernel, tile=tile),
        grid_spec=pltpu.PrefetchScalarGridSpec(
            num_scalar_prefetch=2,
            grid=(1,),
            in_specs=[pl.BlockSpec(memory_space=pl.ANY)],
            out_specs=[pl.BlockSpec(memory_space=pl.ANY)] * peers,
            scratch_shapes=[pltpu.SemaphoreType.DMA((peers, slots))],
        ),
        out_shape=[pair] * peers,
        name="pick",
    )(pos, send, features)
    incoming = [picked[0]] + [None] * (peers - 1)
    for d in order:
        incoming[d] = across(picked[d], "col", n_col, d)
    own_hub = features[:hub_rows]
    same = jnp.stack([own_hub] + [across(own_hub, "row", n_row, d) for d in range(2, n_row, 2)])
    other = across(same, "row", n_row, 1)
    every = jnp.concatenate([same, other])
    slot_of = (which >> 1) + (which & 1) * (n_row // 2)

    block_rows = nodes // 4
    grid = (nodes // block_rows,)

    def rows_of(*shape):
        return pl.BlockSpec((block_rows,) + shape, lambda i, *_: (i, 0))

    adj_spec = pl.BlockSpec((sections, block_rows, hub_rows), lambda i, *_: (0, i, 0))
    raw, deg = pl.pallas_call(
        hub_forward_kernel,
        grid_spec=pltpu.PrefetchScalarGridSpec(
            num_scalar_prefetch=1,
            grid=grid,
            in_specs=[adj_spec]
            + [
                pl.BlockSpec((1, hub_rows, width), lambda i, w, s=s: (w[s], 0, 0))
                for s in range(sections)
            ],
            out_specs=[rows_of(width), rows_of(128)],
        ),
        out_shape=[jax.ShapeDtypeStruct((nodes, width), F32), jax.ShapeDtypeStruct((nodes, 128), F32)],
        compiler_params=params(),
        name="hub_forward",
    )(slot_of, hub_adj[0], *([every] * sections))

    weights = recv_adj[0]
    outs = pl.pallas_call(
        functools.partial(middle_kernel, peers=peers, slots=slots, tile=tile),
        grid_spec=pltpu.PrefetchScalarGridSpec(
            num_scalar_prefetch=3,
            grid=grid,
            in_specs=[
                rows_of(width),
                rows_of(128),
                rows_of(width),
                rows_of(out_width),
                whole(*weights.shape),
                whole(*w_self.shape),
                whole(*w_neigh.shape),
                whole(1, out_width),
            ]
            + [whole(*pair.shape)] * peers,
            out_specs=[rows_of(out_width), rows_of(out_width), rows_of(width)] + [whole(*pair.shape)] * peers,
            scratch_shapes=[
                pltpu.VMEM((block_rows, width), F32),
                pltpu.VMEM((block_rows, 128), F32),
                pltpu.VMEM((nodes, width), BF16),
            ],
        ),
        out_shape=[
            jax.ShapeDtypeStruct((nodes, out_width), BF16),
            jax.ShapeDtypeStruct((nodes, out_width), BF16),
            jax.ShapeDtypeStruct((nodes, width), BF16),
        ]
        + [pair] * peers,
        compiler_params=params(),
        name="middle",
    )(pos, count, dst, raw, deg, features, cotangent, weights, w_self, w_neigh, bias.reshape(1, -1), *incoming)
    output, grad, agg_grad = outs[:3]
    going = outs[3:]
    returned = [going[0]] + [None] * (peers - 1)
    for d in order:
        returned[d] = across(going[d], "col", n_col, d)

    half = jax.ShapeDtypeStruct((n_row // 2, width, hub_rows), BF16)
    even, odd, self_grad = pl.pallas_call(
        hub_backward_kernel,
        grid_spec=pltpu.PrefetchScalarGridSpec(
            num_scalar_prefetch=1,
            grid=grid,
            in_specs=[adj_spec, rows_of(width), rows_of(out_width), whole(*w_self.shape)],
            out_specs=[whole(*half.shape), whole(*half.shape), rows_of(width)],
            scratch_shapes=[pltpu.VMEM((sections, width, hub_rows), F32)],
        ),
        out_shape=[half, half, jax.ShapeDtypeStruct((nodes, width), F32)],
        compiler_params=params(),
        name="hub_backward",
    )(which, hub_adj[0], agg_grad, grad, w_self)
    came = across(odd, "row", n_row, 1)
    block = jax.ShapeDtypeStruct((width, hub_rows), BF16)
    sums = pl.pallas_call(
        pair_add_kernel,
        out_shape=[block] * (n_row // 2),
        compiler_params=params(),
        name="pair_add",
    )(even, came)
    hubs = [sums[0]] + [across(sums[d // 2], "row", n_row, d) for d in range(2, n_row, 2)]

    feature_grad = pl.pallas_call(
        functools.partial(final_kernel, peers=peers, slots=slots, tile=tile),
        grid_spec=pltpu.PrefetchScalarGridSpec(
            num_scalar_prefetch=2,
            grid=grid,
            in_specs=[rows_of(width)] + [whole(*pair.shape)] * peers + [whole(*block.shape)] * len(hubs),
            out_specs=rows_of(width),
            scratch_shapes=[pltpu.VMEM((block_rows, width), F32)],
        ),
        out_shape=jax.ShapeDtypeStruct((nodes, width), BF16),
        compiler_params=params(),
        name="final",
    )(pos, send, self_grad, *returned, *hubs)
    return (output, feature_grad)


def solution(mesh):
    blocks = ("row", "col")
    placed = (
        P(blocks, None),
        P(),
        P(),
        P(),
        P(),
        P(blocks, None, None, None),
        P(blocks, None, None),
        P(blocks, None),
        P(blocks, None, None),
        P(blocks, None, None, None, None),
        P(blocks, None),
    )
    return jax.shard_map(
        functools.partial(shards, n_row=mesh.shape["row"], n_col=mesh.shape["col"]),
        mesh=mesh,
        in_specs=placed,
        out_specs=(P(blocks, None), P(blocks, None)),
        check_vma=False,
    )
```

```python
import functools

import jax
import jax.numpy as jnp
from jax import lax
from jax.experimental import pallas as pl
from jax.experimental.pallas import tpu as pltpu
from jax.sharding import PartitionSpec as P

F32 = jnp.float32
BF16 = jnp.bfloat16
BY_LAST = (((1,), (1,)), ((), ()))
BY_FIRST = (((0,), (0,)), ((), ()))
SMEM = pl.BlockSpec(memory_space=pltpu.SMEM)
ANY = pl.BlockSpec(memory_space=pl.ANY)
HBM = pl.BlockSpec(memory_space=pltpu.HBM)
VMEM = pl.BlockSpec(memory_space=pltpu.VMEM)


def rows_at(index, size):
    return pl.ds(pl.multiple_of(index * size, size), size)


def pick_kernel(send, feats, hub, *rest, tile):
    outs, sems = rest[:-1], rest[-1]
    col = lax.axis_index("col")
    slots = outs[0].shape[0]
    copies = []
    for d, out in enumerate(outs):
        for k in range(slots):
            at = rows_at(send[k, col ^ d], tile)
            copies.append(pltpu.make_async_copy(feats.at[at], out.at[k], sems.at[d * slots + k]))
    copies.append(pltpu.make_async_copy(feats.at[pl.ds(0, hub.shape[0])], hub, sems.at[len(copies)]))
    for copy in copies:
        copy.start()
    for copy in copies:
        copy.wait()


def tile_order(count, dst, order, place, *, peers, slots, tiles):
    landed = jnp.int32(0)
    for p in range(peers):
        for k in range(slots):
            landed = landed | jnp.where(k < count[0, p], jnp.int32(1) << dst[k, p], 0)
    front, back = jnp.int32(0), jnp.int32(tiles - 1)
    for t in range(tiles):
        bit = (landed >> t) & 1
        at = jnp.where(bit == 1, front, back)
        order[at] = jnp.int32(t)
        place[t] = at
        front = front + bit
        back = back - (1 - bit)


def load_kernel(adj, kept, deg, sems, *, chunk):
    sections, nodes, _ = kept.shape
    copies = []
    for i, start in enumerate(range(0, nodes, chunk)):
        at = pl.ds(start, chunk)
        copies.append(pltpu.make_async_copy(adj.at[:, at, :], kept.at[:, at, :], sems.at[i]))
        copies[-1].start()
    for i, copy in enumerate(copies):
        copy.wait()
        at = pl.ds(i * chunk, chunk)
        wide = jnp.concatenate([kept[s, at, :] for s in range(sections)], axis=1).astype(F32)
        lanes = wide[:, 0:128]
        for c in range(128, wide.shape[1], 128):
            lanes = lanes + wide[:, c : c + 128]
        deg[at, :] = jnp.broadcast_to(1.0 + jnp.sum(lanes, axis=1, keepdims=True), (chunk, 128))


def hub_forward_kernel(hub_ids, adj, same, other, raw, blocks, *, chunk):
    row = lax.axis_index("row")
    sections, nodes, hub_rows = adj.shape
    for s in range(sections):
        away = hub_ids[s] ^ row
        at = pl.ds(s * hub_rows, hub_rows)

        @pl.when(away & 1 == 0)
        def _(away=away, at=at):
            blocks[at, :] = same[away >> 1]

        @pl.when(away & 1 == 1)
        def _(away=away, at=at):
            blocks[at, :] = other[away >> 1]

    for start in range(0, nodes, chunk):
        at = pl.ds(start, chunk)
        weights = jnp.concatenate([adj[s, at, :] for s in range(sections)], axis=1)
        raw[at, :] = jnp.dot(weights, blocks[...], preferred_element_type=F32)


def dense(raw, deg, feats, cot, w_self, w_neigh, bias):
    inverse = 1.0 / deg
    inverse = jnp.concatenate([inverse] * (raw.shape[1] // inverse.shape[1]), axis=1)
    agg = (raw * inverse).astype(BF16)
    pre = (
        jnp.dot(feats, w_self[...], preferred_element_type=F32)
        + jnp.dot(agg, w_neigh[...], preferred_element_type=F32)
        + bias[...]
    )
    sig = 0.5 * jnp.tanh(0.5 * pre) + 0.5
    out = (pre * sig).astype(BF16)
    grad = (cot.astype(F32) * sig * (1.0 + pre * (1.0 - sig))).astype(BF16)
    agg_grad = (lax.dot_general(grad, w_neigh[...], BY_LAST, preferred_element_type=F32) * inverse).astype(BF16)
    return out, grad, agg_grad


def landed_kernel(count, dst, raw_in, deg_in, feats, cot, adj, w_self, w_neigh, bias, *rest, peers, slots, tile, group):
    inc = rest[:peers]
    out, grad, agg_grad = rest[peers : peers + 3]
    back = rest[peers + 3 : 2 * peers + 3]
    raw, deg, order, place = rest[2 * peers + 3 :]
    col = lax.axis_index("col")
    tile_order(count, dst, order, place, peers=peers, slots=slots, tiles=raw_in.shape[0] // tile)
    first = raw.shape[0] // tile
    for i in range(first):
        at = rows_at(order[i], tile)
        raw[pl.ds(i * tile, tile), :] = raw_in[at, :]
        deg[pl.ds(i * tile, tile), :] = deg_in[at, :]
    for d in range(peers):
        p = col ^ d
        for k in range(slots):

            @pl.when(k < count[0, p])
            def _(d=d, k=k, p=p):
                at = rows_at(place[dst[k, p]], tile)
                weights = adj[p, k]
                raw[at, :] += jnp.dot(weights, inc[d][k], preferred_element_type=F32)
                deg[at, :] += jnp.sum(weights.astype(F32), axis=1, keepdims=True)

    for start in range(0, first, group):
        here = pl.ds(start * tile, group * tile)
        there = [rows_at(order[i], tile) for i in range(start, start + group)]
        o, g, a = dense(
            raw[here, :],
            deg[here, :],
            jnp.concatenate([feats[at, :] for at in there]),
            jnp.concatenate([cot[at, :] for at in there]),
            w_self,
            w_neigh,
            bias,
        )
        out[here, :] = o
        grad[here, :] = g
        agg_grad[here, :] = a
    for d in range(peers):
        p = col ^ d
        for k in range(slots):
            alive = k < count[0, p]
            at = rows_at(jnp.where(alive, place[dst[k, p]], 0), tile)
            part = lax.dot_general(adj[p, k], agg_grad[at, :], BY_FIRST, preferred_element_type=F32)
            back[d][k] = (part * jnp.where(alive, 1.0, 0.0).astype(F32)).astype(BF16)


def others_kernel(
    count, dst, raw, deg, feats, cot, w_self, w_neigh, bias, out, grad, agg_grad, order, place, *, peers, slots, tile, group
):
    tiles = raw.shape[0] // tile
    first = tiles - out.shape[0] // tile
    tile_order(count, dst, order, place, peers=peers, slots=slots, tiles=tiles)
    for start in range(first, tiles, group):
        here = pl.ds((start - first) * tile, group * tile)
        there = [rows_at(order[i], tile) for i in range(start, start + group)]
        o, g, a = dense(
            *[jnp.concatenate([x[at, :] for at in there]) for x in (raw, deg, feats, cot)], w_self, w_neigh, bias
        )
        out[here, :] = o
        grad[here, :] = g
        agg_grad[here, :] = a


def hub_backward_kernel(count, dst, hub_ids, adj, *rest, peers, slots, tile):
    pieces, (even, odd, agg_grad, order, place) = rest[:-5], rest[-5:]
    row = lax.axis_index("row")
    sections = adj.shape[0]
    tiles = agg_grad.shape[0] // tile
    tile_order(count, dst, order, place, peers=peers, slots=slots, tiles=tiles)
    i = 0
    for piece in pieces:
        for j in range(piece.shape[0] // tile):
            agg_grad[rows_at(order[i], tile), :] = piece[pl.ds(j * tile, tile), :]
            i += 1
    turned = agg_grad[...].T
    owner = [hub_ids[s] ^ row for s in range(sections)]
    for ref in (even, odd):
        ref[...] = jnp.zeros_like(ref)
    parts = [jnp.dot(turned, adj[s], preferred_element_type=F32) for s in range(sections)]
    for s in range(sections):
        total = parts[s]
        for other in range(sections):
            if other != s:
                total = total + parts[other] * jnp.where(owner[other] == owner[s], 1.0, 0.0).astype(F32)

        @pl.when(owner[s] & 1 == 0)
        def _(s=s, total=total):
            even[owner[s] >> 1] = total.astype(BF16)

        @pl.when(owner[s] & 1 == 1)
        def _(s=s, total=total):
            odd[owner[s] >> 1] = total.astype(BF16)


def self_kernel(count, dst, w_self, *rest, peers, slots, tile):
    pieces, (out, self_grad, order, place, sems) = rest[:-5], rest[-5:]
    tiles = self_grad.shape[0] // tile
    tile_order(count, dst, order, place, peers=peers, slots=slots, tiles=tiles)
    copies = []
    i = 0
    for outs, grads in zip(pieces[: len(pieces) // 2], pieces[len(pieces) // 2 :]):
        for j in range(outs.shape[0] // tile):
            copies.append(
                pltpu.make_async_copy(outs.at[pl.ds(j * tile, tile)], out.at[rows_at(order[i], tile)], sems.at[i])
            )
            copies[-1].start()
            i += 1
    i = 0
    for grads in pieces[len(pieces) // 2 :]:
        through = lax.dot_general(grads[...], w_self[...], BY_LAST, preferred_element_type=F32)
        for j in range(grads.shape[0] // tile):
            self_grad[rows_at(order[i], tile), :] = through[j * tile : (j + 1) * tile]
            i += 1
    for copy in copies:
        copy.wait()


def pair_add_kernel(even, came, *outs):
    for e, out in enumerate(outs):
        out[...] = (even[e].astype(F32) + came[e].astype(F32)).astype(BF16)


def final_kernel(send, self_grad, *rest, peers, slots, tile, chunk):
    back, hub, (out, total, done, sems) = rest[:peers], rest[peers:-4], rest[-4:]
    col = lax.axis_index("col")
    total[...] = self_grad[...]
    for d in range(peers):
        for k in range(slots):
            total[rows_at(send[k, col ^ d], tile), :] += back[d][k].astype(F32)
    come = hub[0][...].astype(F32)
    for h in hub[1:]:
        come = come + h[...].astype(F32)
    total[0 : come.shape[1], :] += come.T
    copies = []
    for i, start in enumerate(range(0, total.shape[0], chunk)):
        at = pl.ds(start, chunk)
        done[at, :] = total[at, :].astype(BF16)
        copies.append(pltpu.make_async_copy(done.at[at], out.at[at], sems.at[i]))
        copies[-1].start()
    for copy in copies:
        copy.wait()


def shards(
    features, w_self, w_neigh, bias, hub_ids, hub_adj, send_tile, recv_count, recv_dst, recv_adj, cotangent, *, n_row, n_col
):
    nodes, width = features.shape
    sections, hub_rows = hub_ids.shape[0], hub_adj.shape[3]
    peers, slots, tile = recv_adj.shape[1], recv_adj.shape[2], recv_adj.shape[3]
    out_width = w_self.shape[1]
    tiles = nodes // tile
    first = min(peers * slots, tiles)
    group = 4
    send, count, dst = send_tile.swapaxes(1, 2)[0], recv_count, recv_dst.swapaxes(1, 2)[0]
    adj, weights, bias = hub_adj[0], recv_adj[0], bias.reshape(1, -1)
    params = pltpu.CompilerParams(vmem_limit_bytes=24 * 1024 * 1024)
    shape = jax.ShapeDtypeStruct
    sizes = dict(peers=peers, slots=slots, tile=tile)

    def cost(flops):
        return pl.CostEstimate(flops=flops, transcendentals=0, bytes_accessed=8 * nodes * width)

    def across(x, axis, size, d):
        return lax.ppermute(x, axis, [(i, i ^ d) for i in range(size)])

    order = exchange_order(n_col)
    pair = shape((slots, tile, width), BF16)
    own_hub, *picked = pl.pallas_call(
        functools.partial(pick_kernel, tile=tile),
        in_specs=[SMEM, HBM],
        out_specs=[VMEM] * (peers + 1),
        scratch_shapes=[pltpu.SemaphoreType.DMA((peers * slots + 1,))],
        out_shape=[shape((hub_rows, width), BF16)] + [pair] * peers,
        compiler_params=params,
        name="pick",
    )(pltpu.with_memory_space_constraint(send, pltpu.HBM), pltpu.with_memory_space_constraint(features, pltpu.HBM))
    incoming = [picked[0]] + [None] * (peers - 1)
    for d in order:
        incoming[d] = across(picked[d], "col", n_col, d)
    same = jnp.stack([own_hub] + [across(own_hub, "row", n_row, d) for d in range(2, n_row, 2)])
    other = across(same, "row", n_row, 1)

    adj, deg = pl.pallas_call(
        functools.partial(load_kernel, chunk=nodes // 8),
        in_specs=[HBM],
        out_specs=[VMEM, VMEM],
        scratch_shapes=[pltpu.SemaphoreType.DMA((8,))],
        out_shape=[shape(adj.shape, BF16), shape((nodes, 128), F32)],
        compiler_params=params,
        name="load",
    )(pltpu.with_memory_space_constraint(adj, pltpu.HBM))
    raw = pl.pallas_call(
        functools.partial(hub_forward_kernel, chunk=256),
        in_specs=[SMEM, VMEM, VMEM, VMEM],
        out_specs=VMEM,
        scratch_shapes=[pltpu.VMEM((sections * hub_rows, width), BF16)],
        out_shape=shape((nodes, width), F32),
        compiler_params=params,
        cost_estimate=cost(2 * sections * nodes * hub_rows * width),
        name="hub_forward",
    )(hub_ids, adj, same, other)

    tables = [pltpu.SMEM((tiles,), jnp.int32), pltpu.SMEM((tiles,), jnp.int32)]

    def results(number):
        return [shape((number * tile, n), BF16) for n in (out_width, out_width, width)]

    others = []
    if first < tiles:
        others = pl.pallas_call(
            functools.partial(others_kernel, group=group, **sizes),
            in_specs=[SMEM, SMEM] + [VMEM] * 7,
            out_specs=[VMEM] * 3,
            scratch_shapes=tables,
            out_shape=results(tiles - first),
            compiler_params=params,
            name="others",
        )(count, dst, raw, deg, features, cotangent, w_self, w_neigh, bias)
    landed = pl.pallas_call(
        functools.partial(landed_kernel, group=group, **sizes),
        in_specs=[SMEM, SMEM] + [VMEM] * (8 + peers),
        out_specs=[VMEM] * (3 + peers),
        scratch_shapes=[pltpu.VMEM((first * tile, width), F32), pltpu.VMEM((first * tile, 128), F32)] + tables,
        out_shape=results(first) + [pair] * peers,
        compiler_params=params,
        name="landed",
    )(count, dst, raw, deg, features, cotangent, weights, w_self, w_neigh, bias, *incoming)
    outs, grads, agg_grads = zip(*([landed[:3]] + ([others] if others else [])))
    going = landed[3:]
    returned = [going[0]] + [None] * (peers - 1)
    for d in order:
        returned[d] = across(going[d], "col", n_col, d)

    half = shape((n_row // 2, width, hub_rows), BF16)
    even, odd = pl.pallas_call(
        functools.partial(hub_backward_kernel, **sizes),
        in_specs=[SMEM] * 3 + [VMEM] * (1 + len(agg_grads)),
        out_specs=[VMEM] * 2,
        scratch_shapes=[pltpu.VMEM((nodes, width), BF16)] + tables,
        out_shape=[half, half],
        compiler_params=params,
        cost_estimate=cost(2 * sections * nodes * hub_rows * width),
        name="hub_backward",
    )(count, dst, hub_ids, adj, *agg_grads)
    came = across(odd, "row", n_row, 1)
    output, self_grad = pl.pallas_call(
        functools.partial(self_kernel, **sizes),
        in_specs=[SMEM] * 2 + [VMEM] * (1 + 2 * len(outs)),
        out_specs=[HBM, VMEM],
        scratch_shapes=tables + [pltpu.SemaphoreType.DMA((tiles,))],
        out_shape=[shape((nodes, out_width), BF16), shape((nodes, width), F32)],
        compiler_params=params,
        name="self",
    )(count, dst, w_self, *outs, *grads)
    block = shape((width, hub_rows), BF16)
    sums = pl.pallas_call(
        pair_add_kernel,
        out_shape=[block] * (n_row // 2),
        compiler_params=params,
        name="pair_add",
    )(even, came)
    hubs = [sums[0]] + [across(sums[d // 2], "row", n_row, d) for d in range(2, n_row, 2)]

    feature_grad = pl.pallas_call(
        functools.partial(final_kernel, chunk=nodes // 4, **sizes),
        in_specs=[SMEM] + [VMEM] * (1 + peers + len(hubs)),
        out_specs=ANY,
        scratch_shapes=[
            pltpu.VMEM((nodes, width), F32),
            pltpu.VMEM((nodes, width), BF16),
            pltpu.SemaphoreType.DMA((4,)),
        ],
        out_shape=shape((nodes, width), BF16),
        compiler_params=params,
        name="final",
    )(send, self_grad, *returned, *hubs)
    return (output, feature_grad)


def exchange_order(n_col):
    return sorted(range(1, n_col), key=lambda d: (d != n_col // 2, -d))


def solution(mesh):
    blocks = ("row", "col")
    placed = (
        P(blocks, None),
        P(),
        P(),
        P(),
        P(),
        P(blocks, None, None, None),
        P(blocks, None, None),
        P(blocks, None),
        P(blocks, None, None),
        P(blocks, None, None, None, None),
        P(blocks, None),
    )
    n_row, n_col = mesh.shape["row"], mesh.shape["col"]

    def body(*args):
        return shards(*args, n_row=n_row, n_col=n_col)

    return jax.shard_map(
        body, mesh=mesh, in_specs=placed, out_specs=(P(blocks, None), P(blocks, None)), check_vma=False
    )
```

```python
import functools

import jax
import jax.numpy as jnp
from jax import lax
from jax.experimental import pallas as pl
from jax.experimental.pallas import tpu as pltpu
from jax.sharding import PartitionSpec as P

F32 = jnp.float32
BF16 = jnp.bfloat16
BY_LAST = (((1,), (1,)), ((), ()))
BY_FIRST = (((0,), (0,)), ((), ()))
SMEM = pl.BlockSpec(memory_space=pltpu.SMEM)
ANY = pl.BlockSpec(memory_space=pl.ANY)
HBM = pl.BlockSpec(memory_space=pltpu.HBM)
VMEM = pl.BlockSpec(memory_space=pltpu.VMEM)


def rows_at(index, size):
    return pl.ds(pl.multiple_of(index * size, size), size)


def pick_kernel(send, feats, hub, *rest, tile):
    outs, sems = rest[:-1], rest[-1]
    col = lax.axis_index("col")
    slots = outs[0].shape[0]
    copies = []
    for d, out in enumerate(outs):
        for k in range(slots):
            at = rows_at(send[k, col ^ d], tile)
            copies.append(pltpu.make_async_copy(feats.at[at], out.at[k], sems.at[d * slots + k]))
    copies.append(pltpu.make_async_copy(feats.at[pl.ds(0, hub.shape[0])], hub, sems.at[len(copies)]))
    for copy in copies:
        copy.start()
    for copy in copies:
        copy.wait()


def tile_order(count, dst, order, place, *, peers, slots, tiles):
    landed = jnp.int32(0)
    for p in range(peers):
        for k in range(slots):
            landed = landed | jnp.where(k < count[0, p], jnp.int32(1) << dst[k, p], 0)
    front, back = jnp.int32(0), jnp.int32(tiles - 1)
    for t in range(tiles):
        bit = (landed >> t) & 1
        at = jnp.where(bit == 1, front, back)
        order[at] = jnp.int32(t)
        place[t] = at
        front = front + bit
        back = back - (1 - bit)


def load_kernel(adj, kept, deg, sems, *, chunk):
    sections, nodes, _ = kept.shape
    copies = []
    for i, start in enumerate(range(0, nodes, chunk)):
        at = pl.ds(start, chunk)
        copies.append(pltpu.make_async_copy(adj.at[:, at, :], kept.at[:, at, :], sems.at[i]))
        copies[-1].start()
    for i, copy in enumerate(copies):
        copy.wait()
        at = pl.ds(i * chunk, chunk)
        wide = jnp.concatenate([kept[s, at, :] for s in range(sections)], axis=1).astype(F32)
        lanes = wide[:, 0:128]
        for c in range(128, wide.shape[1], 128):
            lanes = lanes + wide[:, c : c + 128]
        deg[at, :] = jnp.broadcast_to(1.0 + jnp.sum(lanes, axis=1, keepdims=True), (chunk, 128))


def dense(raw, deg, feats, cot, w_self, w_neigh, bias):
    inverse = 1.0 / deg
    inverse = jnp.concatenate([inverse] * (raw.shape[1] // inverse.shape[1]), axis=1)
    agg = (raw * inverse).astype(BF16)
    pre = (
        jnp.dot(feats, w_self[...], preferred_element_type=F32)
        + jnp.dot(agg, w_neigh[...], preferred_element_type=F32)
        + bias[...]
    )
    sig = 0.5 * jnp.tanh(0.5 * pre) + 0.5
    out = (pre * sig).astype(BF16)
    grad = (cot.astype(F32) * sig * (1.0 + pre * (1.0 - sig))).astype(BF16)
    agg_grad = (lax.dot_general(grad, w_neigh[...], BY_LAST, preferred_element_type=F32) * inverse).astype(BF16)
    return out, grad, agg_grad


def forward_kernel(
    count, dst, hub_ids, adj, same, other, deg, feats, cot, w_self, w_neigh, bias,
    raw, *rest, peers, slots, tile, chunk, group
):
    results, (blocks, order, place) = rest[:-3], rest[-3:]
    row = lax.axis_index("row")
    sections, nodes, hub_rows = adj.shape
    for s in range(sections):
        away = hub_ids[s] ^ row
        at = pl.ds(s * hub_rows, hub_rows)

        @pl.when(away & 1 == 0)
        def _(away=away, at=at):
            blocks[at, :] = same[away >> 1]

        @pl.when(away & 1 == 1)
        def _(away=away, at=at):
            blocks[at, :] = other[away >> 1]

    tiles = nodes // tile
    if results:
        tile_order(count, dst, order, place, peers=peers, slots=slots, tiles=tiles)
    for start in range(0, nodes, chunk):
        at = pl.ds(start, chunk)
        weights = jnp.concatenate([adj[s, at, :] for s in range(sections)], axis=1)
        raw[at, :] = jnp.dot(weights, blocks[...], preferred_element_type=F32)
    if results:
        out, grad, turned = results
        first = tiles - out.shape[0] // tile
        for start in range(first, tiles, group):
            here = pl.ds((start - first) * tile, group * tile)
            there = [rows_at(order[i], tile) for i in range(start, start + group)]
            o, g, a = dense(
                *[jnp.concatenate([x[at, :] for at in there]) for x in (raw, deg, feats, cot)], w_self, w_neigh, bias
            )
            out[here, :] = o
            grad[here, :] = g
            turned[:, here] = a.T


def landed_kernel(count, dst, raw_in, deg_in, feats, cot, adj, w_self, w_neigh, bias, *rest, peers, slots, tile, group):
    inc = rest[:peers]
    out, grad, turned = rest[peers : peers + 3]
    back = rest[peers + 3 : 2 * peers + 3]
    raw, deg, agg_grad, order, place = rest[2 * peers + 3 :]
    col = lax.axis_index("col")
    tile_order(count, dst, order, place, peers=peers, slots=slots, tiles=raw_in.shape[0] // tile)
    first = raw.shape[0] // tile
    for i in range(first):
        at = rows_at(order[i], tile)
        raw[pl.ds(i * tile, tile), :] = raw_in[at, :]
        deg[pl.ds(i * tile, tile), :] = deg_in[at, :]
    parts = []
    for d in range(peers):
        p = col ^ d
        for k in range(slots):
            weights = adj[p, k]
            parts.append(
                (
                    k < count[0, p],
                    dst[k, p],
                    jnp.dot(weights, inc[d][k], preferred_element_type=F32),
                    jnp.sum(weights.astype(F32), axis=1, keepdims=True),
                )
            )
    for alive, target, part, lanes in parts:
        at = rows_at(jnp.where(alive, place[target], 0), tile)
        scale = jnp.where(alive, 1.0, 0.0).astype(F32)
        raw[at, :] += part * scale
        deg[at, :] += lanes * scale
    for start in range(0, first, group):
        here = pl.ds(start * tile, group * tile)
        there = [rows_at(order[i], tile) for i in range(start, start + group)]
        o, g, a = dense(
            raw[here, :],
            deg[here, :],
            jnp.concatenate([feats[at, :] for at in there]),
            jnp.concatenate([cot[at, :] for at in there]),
            w_self,
            w_neigh,
            bias,
        )
        out[here, :] = o
        grad[here, :] = g
        agg_grad[here, :] = a
        turned[:, here] = a.T
    for d in range(peers):
        p = col ^ d
        for k in range(slots):
            alive = k < count[0, p]
            at = rows_at(jnp.where(alive, place[dst[k, p]], 0), tile)
            part = lax.dot_general(adj[p, k], agg_grad[at, :], BY_FIRST, preferred_element_type=F32)
            back[d][k] = (part * jnp.where(alive, 1.0, 0.0).astype(F32)).astype(BF16)


def hub_backward_kernel(count, dst, hub_ids, adj, *rest, peers, slots, tile):
    pieces, (even, odd, acc, order, place) = rest[:-5], rest[-5:]
    row = lax.axis_index("row")
    sections, nodes, _ = adj.shape
    tile_order(count, dst, order, place, peers=peers, slots=slots, tiles=nodes // tile)
    there = [rows_at(order[i], tile) for i in range(nodes // tile)]
    acc[...] = jnp.zeros_like(acc)
    for s in range(sections):
        turned = jnp.concatenate([piece[...] for piece in pieces], axis=1)
        weights = jnp.concatenate([adj[s, at, :] for at in there])
        acc[hub_ids[s] ^ row] += jnp.dot(turned, weights, preferred_element_type=F32)
    for e in range(even.shape[0]):
        even[e] = acc[2 * e].astype(BF16)
        odd[e] = acc[2 * e + 1].astype(BF16)


def self_kernel(count, dst, w_self, *rest, peers, slots, tile):
    pieces, (out, self_grad, order, place, sems) = rest[:-5], rest[-5:]
    tiles = self_grad.shape[0] // tile
    tile_order(count, dst, order, place, peers=peers, slots=slots, tiles=tiles)
    copies = []
    i = 0
    for outs, grads in zip(pieces[: len(pieces) // 2], pieces[len(pieces) // 2 :]):
        for j in range(outs.shape[0] // tile):
            copies.append(
                pltpu.make_async_copy(outs.at[pl.ds(j * tile, tile)], out.at[rows_at(order[i], tile)], sems.at[i])
            )
            copies[-1].start()
            i += 1
    i = 0
    for grads in pieces[len(pieces) // 2 :]:
        through = lax.dot_general(grads[...], w_self[...], BY_LAST, preferred_element_type=F32)
        for j in range(grads.shape[0] // tile):
            self_grad[rows_at(order[i], tile), :] = through[j * tile : (j + 1) * tile]
            i += 1
    for copy in copies:
        copy.wait()


def pair_add_kernel(even, came, *outs):
    for e, out in enumerate(outs):
        out[...] = (even[e].astype(F32) + came[e].astype(F32)).astype(BF16)


def tiles_kernel(send, self_grad, *rest, peers, slots, tile, chunk):
    back, (out, head, total, done, sems) = rest[:peers], rest[peers:]
    col = lax.axis_index("col")
    total[...] = self_grad[...]
    for d in range(peers):
        for k in range(slots):
            total[rows_at(send[k, col ^ d], tile), :] += back[d][k].astype(F32)
    head[...] = total[pl.ds(0, head.shape[0]), :]
    copies = []
    for i, start in enumerate(range(head.shape[0], total.shape[0], chunk)):
        at = pl.ds(start, chunk)
        done[at, :] = total[at, :].astype(BF16)
        copies.append(pltpu.make_async_copy(done.at[at], out.at[at], sems.at[i]))
        copies[-1].start()
    for copy in copies:
        copy.wait()


def head_kernel(head, *rest):
    hub, (_, out, done, sem) = rest[:-4], rest[-4:]
    come = hub[0][...].astype(F32)
    for h in hub[1:]:
        come = come + h[...].astype(F32)
    done[...] = (head[...] + come.T).astype(BF16)
    copy = pltpu.make_async_copy(done, out.at[pl.ds(0, done.shape[0])], sem)
    copy.start()
    copy.wait()


def shards(
    features, w_self, w_neigh, bias, hub_ids, hub_adj, send_tile, recv_count, recv_dst, recv_adj, cotangent, *, n_row, n_col
):
    nodes, width = features.shape
    sections, hub_rows = hub_ids.shape[0], hub_adj.shape[3]
    peers, slots, tile = recv_adj.shape[1], recv_adj.shape[2], recv_adj.shape[3]
    out_width = w_self.shape[1]
    tiles = nodes // tile
    first = min(peers * slots, tiles)
    group = 4
    send, count, dst = send_tile.swapaxes(1, 2)[0], recv_count, recv_dst.swapaxes(1, 2)[0]
    adj, weights, bias = hub_adj[0], recv_adj[0], bias.reshape(1, -1)
    params = pltpu.CompilerParams(vmem_limit_bytes=24 * 1024 * 1024)
    shape = jax.ShapeDtypeStruct
    sizes = dict(peers=peers, slots=slots, tile=tile)

    def cost(flops):
        return pl.CostEstimate(flops=flops, transcendentals=0, bytes_accessed=8 * nodes * width)

    def across(x, axis, size, d):
        return lax.ppermute(x, axis, [(i, i ^ d) for i in range(size)])

    order = exchange_order(n_col)
    pair = shape((slots, tile, width), BF16)
    own_hub, *picked = pl.pallas_call(
        functools.partial(pick_kernel, tile=tile),
        in_specs=[SMEM, HBM],
        out_specs=[VMEM] * (peers + 1),
        scratch_shapes=[pltpu.SemaphoreType.DMA((peers * slots + 1,))],
        out_shape=[shape((hub_rows, width), BF16)] + [pair] * peers,
        compiler_params=params,
        name="pick",
    )(pltpu.with_memory_space_constraint(send, pltpu.HBM), pltpu.with_memory_space_constraint(features, pltpu.HBM))
    incoming = [picked[0]] + [None] * (peers - 1)
    for d in order:
        incoming[d] = across(picked[d], "col", n_col, d)
    same = jnp.stack([own_hub] + [across(own_hub, "row", n_row, d) for d in range(2, n_row, 2)])
    other = across(same, "row", n_row, 1)

    adj, deg = pl.pallas_call(
        functools.partial(load_kernel, chunk=nodes // 8),
        in_specs=[HBM],
        out_specs=[VMEM, VMEM],
        scratch_shapes=[pltpu.SemaphoreType.DMA((8,))],
        out_shape=[shape(adj.shape, BF16), shape((nodes, 128), F32)],
        compiler_params=params,
        name="load",
    )(pltpu.with_memory_space_constraint(adj, pltpu.HBM))
    tables = [pltpu.SMEM((tiles,), jnp.int32), pltpu.SMEM((tiles,), jnp.int32)]

    def results(number):
        if not number:
            return []
        return [shape((number * tile, out_width), BF16)] * 2 + [shape((width, number * tile), BF16)]

    raw, *others = pl.pallas_call(
        functools.partial(forward_kernel, chunk=256, group=group, **sizes),
        in_specs=[SMEM] * 3 + [VMEM] * 9,
        out_specs=[VMEM] * (1 + len(results(tiles - first))),
        scratch_shapes=[pltpu.VMEM((sections * hub_rows, width), BF16)] + tables,
        out_shape=[shape((nodes, width), F32)] + results(tiles - first),
        compiler_params=params,
        cost_estimate=cost(2 * sections * nodes * hub_rows * width),
        name="forward",
    )(count, dst, hub_ids, adj, same, other, deg, features, cotangent, w_self, w_neigh, bias)
    landed = pl.pallas_call(
        functools.partial(landed_kernel, group=group, **sizes),
        in_specs=[SMEM, SMEM] + [VMEM] * (8 + peers),
        out_specs=[VMEM] * (3 + peers),
        scratch_shapes=[pltpu.VMEM((first * tile, n), t) for n, t in ((width, F32), (128, F32), (width, BF16))]
        + tables,
        out_shape=results(first) + [pair] * peers,
        compiler_params=params,
        name="landed",
    )(count, dst, raw, deg, features, cotangent, weights, w_self, w_neigh, bias, *incoming)
    outs, grads, turned = zip(*([landed[:3]] + ([others] if others else [])))
    going = landed[3:]
    returned = [going[0]] + [None] * (peers - 1)
    for d in order:
        returned[d] = across(going[d], "col", n_col, d)

    half = shape((n_row // 2, width, hub_rows), BF16)
    even, odd = pl.pallas_call(
        functools.partial(hub_backward_kernel, **sizes),
        in_specs=[SMEM] * 3 + [VMEM] * (1 + len(turned)),
        out_specs=[VMEM] * 2,
        scratch_shapes=[pltpu.VMEM((n_row, width, hub_rows), F32)] + tables,
        out_shape=[half, half],
        compiler_params=params,
        cost_estimate=cost(2 * sections * nodes * hub_rows * width),
        name="hub_backward",
    )(count, dst, hub_ids, adj, *turned)
    came = across(odd, "row", n_row, 1)
    output, self_grad = pl.pallas_call(
        functools.partial(self_kernel, **sizes),
        in_specs=[SMEM] * 2 + [VMEM] * (1 + 2 * len(outs)),
        out_specs=[HBM, VMEM],
        scratch_shapes=tables + [pltpu.SemaphoreType.DMA((tiles,))],
        out_shape=[shape((nodes, out_width), BF16), shape((nodes, width), F32)],
        compiler_params=params,
        name="self",
    )(count, dst, w_self, *outs, *grads)
    block = shape((width, hub_rows), BF16)
    sums = pl.pallas_call(
        pair_add_kernel,
        out_shape=[block] * (n_row // 2),
        compiler_params=params,
        name="pair_add",
    )(even, came)
    hubs = [sums[0]] + [across(sums[d // 2], "row", n_row, d) for d in range(2, n_row, 2)]

    chunk = 2 * tile
    feature_grad, head = pl.pallas_call(
        functools.partial(tiles_kernel, chunk=chunk, **sizes),
        in_specs=[SMEM] + [VMEM] * (1 + peers),
        out_specs=[HBM, VMEM],
        scratch_shapes=[
            pltpu.VMEM((nodes, width), F32),
            pltpu.VMEM((nodes, width), BF16),
            pltpu.SemaphoreType.DMA(((nodes - hub_rows) // chunk,)),
        ],
        out_shape=[shape((nodes, width), BF16), shape((hub_rows, width), F32)],
        compiler_params=params,
        name="tiles_done",
    )(send, self_grad, *returned)
    feature_grad = pl.pallas_call(
        head_kernel,
        in_specs=[VMEM] * (1 + len(hubs)) + [HBM],
        out_specs=HBM,
        scratch_shapes=[pltpu.VMEM((hub_rows, width), BF16), pltpu.SemaphoreType.DMA],
        out_shape=shape((nodes, width), BF16),
        input_output_aliases={1 + len(hubs): 0},
        compiler_params=params,
        name="head",
    )(head, *hubs, feature_grad)
    return (output, feature_grad)


def exchange_order(n_col):
    return sorted(range(1, n_col), key=lambda d: (d != n_col // 2, d))


def solution(mesh):
    blocks = ("row", "col")
    placed = (
        P(blocks, None),
        P(),
        P(),
        P(),
        P(),
        P(blocks, None, None, None),
        P(blocks, None, None),
        P(blocks, None),
        P(blocks, None, None),
        P(blocks, None, None, None, None),
        P(blocks, None),
    )
    n_row, n_col = mesh.shape["row"], mesh.shape["col"]

    def body(*args):
        return shards(*args, n_row=n_row, n_col=n_col)

    return jax.shard_map(
        body, mesh=mesh, in_specs=placed, out_specs=(P(blocks, None), P(blocks, None)), check_vma=False
    )
```

```python
import functools

import jax
import jax.numpy as jnp
from jax import lax
from jax.experimental import pallas as pl
from jax.experimental.pallas import tpu as pltpu
from jax.sharding import PartitionSpec as P

F32 = jnp.float32
BF16 = jnp.bfloat16
BY_LAST = (((1,), (1,)), ((), ()))
BY_FIRST = (((0,), (0,)), ((), ()))
SMEM = pl.BlockSpec(memory_space=pltpu.SMEM)
ANY = pl.BlockSpec(memory_space=pl.ANY)
HBM = pl.BlockSpec(memory_space=pltpu.HBM)
VMEM = pl.BlockSpec(memory_space=pltpu.VMEM)


def rows_at(index, size):
    return pl.ds(pl.multiple_of(index * size, size), size)


def pick_kernel(send, feats, hub, *rest, tile):
    outs, sems = rest[:-1], rest[-1]
    col = lax.axis_index("col")
    slots = outs[0].shape[0]
    copies = []
    for d, out in enumerate(outs):
        for k in range(slots):
            at = rows_at(send[k, col ^ d], tile)
            copies.append(pltpu.make_async_copy(feats.at[at], out.at[k], sems.at[d * slots + k]))
    copies.append(pltpu.make_async_copy(feats.at[pl.ds(0, hub.shape[0])], hub, sems.at[len(copies)]))
    for copy in copies:
        copy.start()
    for copy in copies:
        copy.wait()


def tile_order(count, dst, order, place, *, peers, slots, tiles):
    landed = jnp.int32(0)
    for p in range(peers):
        for k in range(slots):
            landed = landed | jnp.where(k < count[0, p], jnp.int32(1) << dst[k, p], 0)
    front, back = jnp.int32(0), jnp.int32(tiles - 1)
    for t in range(tiles):
        bit = (landed >> t) & 1
        at = jnp.where(bit == 1, front, back)
        order[at] = jnp.int32(t)
        place[t] = at
        front = front + bit
        back = back - (1 - bit)


def early_kernel(count, dst, feats, w_self, bias, order, place, own, *, peers, slots, tile):
    tile_order(count, dst, order, place, peers=peers, slots=slots, tiles=feats.shape[0] // tile)
    own[...] = jnp.dot(feats[...], w_self[...], preferred_element_type=F32) + bias[...]


def dense(raw, deg, own, cot, w_neigh):
    inverse = 1.0 / deg
    inverse = jnp.concatenate([inverse] * (raw.shape[1] // inverse.shape[1]), axis=1)
    agg = (raw * inverse).astype(BF16)
    pre = own + jnp.dot(agg, w_neigh[...], preferred_element_type=F32)
    sig = 0.5 * jnp.tanh(0.5 * pre) + 0.5
    out = (pre * sig).astype(BF16)
    grad = (cot.astype(F32) * sig * (1.0 + pre * (1.0 - sig))).astype(BF16)
    agg_grad = (lax.dot_general(grad, w_neigh[...], BY_LAST, preferred_element_type=F32) * inverse).astype(BF16)
    return out, grad, agg_grad


def forward_kernel(
    order, hub_ids, adj, same, other, own, cot, w_neigh, raw, deg, *rest, tile, chunk, group
):
    results, blocks = rest[:-1], rest[-1]
    row = lax.axis_index("row")
    sections, nodes, hub_rows = adj.shape
    for s in range(sections):
        away = hub_ids[s] ^ row
        at = pl.ds(s * hub_rows, hub_rows)

        @pl.when(away & 1 == 0)
        def _(away=away, at=at):
            blocks[at, :] = same[away >> 1]

        @pl.when(away & 1 == 1)
        def _(away=away, at=at):
            blocks[at, :] = other[away >> 1]

    tiles = nodes // tile
    for start in range(0, nodes, chunk):
        at = pl.ds(start, chunk)
        weights = jnp.concatenate([adj[s, at, :] for s in range(sections)], axis=1)
        raw[at, :] = jnp.dot(weights, blocks[...], preferred_element_type=F32)
        wide = weights.astype(F32)
        lanes = wide[:, 0:128]
        for c in range(128, wide.shape[1], 128):
            lanes = lanes + wide[:, c : c + 128]
        deg[at, :] = jnp.broadcast_to(1.0 + jnp.sum(lanes, axis=1, keepdims=True), (chunk, 128))
    if results:
        out, grad, turned = results
        first = tiles - out.shape[0] // tile
        for start in range(first, tiles, group):
            here = pl.ds((start - first) * tile, group * tile)
            there = [rows_at(order[i], tile) for i in range(start, start + group)]
            o, g, a = dense(
                *[jnp.concatenate([x[at, :] for at in there]) for x in (raw, deg, own, cot)], w_neigh
            )
            out[here, :] = o
            grad[here, :] = g
            turned[:, here] = a.T


def landed_kernel(count, dst, order, place, raw_in, deg_in, own, cot, adj, w_neigh, *rest, peers, slots, tile, group):
    inc = rest[:peers]
    out, grad, turned = rest[peers : peers + 3]
    back = rest[peers + 3 : 2 * peers + 3]
    raw, deg, agg_grad = rest[2 * peers + 3 :]
    col = lax.axis_index("col")
    first = raw.shape[0] // tile
    for i in range(first):
        at = rows_at(order[i], tile)
        raw[pl.ds(i * tile, tile), :] = raw_in[at, :]
        deg[pl.ds(i * tile, tile), :] = deg_in[at, :]
    parts = []
    for d in range(peers):
        p = col ^ d
        for k in range(slots):
            weights = adj[p, k]
            parts.append(
                (
                    k < count[0, p],
                    dst[k, p],
                    jnp.dot(weights, inc[d][k], preferred_element_type=F32),
                    jnp.sum(weights.astype(F32), axis=1, keepdims=True),
                )
            )
    for alive, target, part, lanes in parts:
        at = rows_at(jnp.where(alive, place[target], 0), tile)
        scale = jnp.where(alive, 1.0, 0.0).astype(F32)
        raw[at, :] += part * scale
        deg[at, :] += lanes * scale
    for start in range(0, first, group):
        here = pl.ds(start * tile, group * tile)
        there = [rows_at(order[i], tile) for i in range(start, start + group)]
        o, g, a = dense(
            raw[here, :],
            deg[here, :],
            jnp.concatenate([own[at, :] for at in there]),
            jnp.concatenate([cot[at, :] for at in there]),
            w_neigh,
        )
        out[here, :] = o
        grad[here, :] = g
        agg_grad[here, :] = a
        turned[:, here] = a.T
    for d in range(peers):
        p = col ^ d
        for k in range(slots):
            alive = k < count[0, p]
            at = rows_at(jnp.where(alive, place[dst[k, p]], 0), tile)
            part = lax.dot_general(adj[p, k], agg_grad[at, :], BY_FIRST, preferred_element_type=F32)
            back[d][k] = (part * jnp.where(alive, 1.0, 0.0).astype(F32)).astype(BF16)


def hub_backward_kernel(order, hub_ids, adj, *rest, tile):
    pieces, (even, odd, acc) = rest[:-3], rest[-3:]
    row = lax.axis_index("row")
    sections, nodes, _ = adj.shape
    there = [rows_at(order[i], tile) for i in range(nodes // tile)]
    acc[...] = jnp.zeros_like(acc)
    for s in range(sections):
        turned = jnp.concatenate([piece[...] for piece in pieces], axis=1)
        weights = jnp.concatenate([adj[s, at, :] for at in there])
        acc[hub_ids[s] ^ row] += jnp.dot(turned, weights, preferred_element_type=F32)
    for e in range(even.shape[0]):
        even[e] = acc[2 * e].astype(BF16)
        odd[e] = acc[2 * e + 1].astype(BF16)


def self_kernel(order, w_self, *rest, tile):
    pieces, (out, self_grad, sems) = rest[:-3], rest[-3:]
    copies = []
    i = 0
    for outs, grads in zip(pieces[: len(pieces) // 2], pieces[len(pieces) // 2 :]):
        for j in range(outs.shape[0] // tile):
            copies.append(
                pltpu.make_async_copy(outs.at[pl.ds(j * tile, tile)], out.at[rows_at(order[i], tile)], sems.at[i])
            )
            copies[-1].start()
            i += 1
    i = 0
    for grads in pieces[len(pieces) // 2 :]:
        through = lax.dot_general(grads[...], w_self[...], BY_LAST, preferred_element_type=F32)
        for j in range(grads.shape[0] // tile):
            self_grad[rows_at(order[i], tile), :] = through[j * tile : (j + 1) * tile]
            i += 1
    for copy in copies:
        copy.wait()


def pair_add_kernel(even, came, *outs):
    for e, out in enumerate(outs):
        out[...] = (even[e].astype(F32) + came[e].astype(F32)).astype(BF16)


def tiles_kernel(send, self_grad, *rest, peers, slots, tile, chunk):
    back, (out, head, total, done, sems) = rest[:peers], rest[peers:]
    col = lax.axis_index("col")
    total[...] = self_grad[...]
    for d in range(peers):
        for k in range(slots):
            total[rows_at(send[k, col ^ d], tile), :] += back[d][k].astype(F32)
    head[...] = total[pl.ds(0, head.shape[0]), :]
    copies = []
    for i, start in enumerate(range(head.shape[0], total.shape[0], chunk)):
        at = pl.ds(start, chunk)
        done[at, :] = total[at, :].astype(BF16)
        copies.append(pltpu.make_async_copy(done.at[at], out.at[at], sems.at[i]))
        copies[-1].start()
    for copy in copies:
        copy.wait()


def head_kernel(head, *rest):
    hub, (_, out, done, sem) = rest[:-4], rest[-4:]
    come = hub[0][...].astype(F32)
    for h in hub[1:]:
        come = come + h[...].astype(F32)
    done[...] = (head[...] + come.T).astype(BF16)
    copy = pltpu.make_async_copy(done, out.at[pl.ds(0, done.shape[0])], sem)
    copy.start()
    copy.wait()


def shards(
    features, w_self, w_neigh, bias, hub_ids, hub_adj, send_tile, recv_count, recv_dst, recv_adj, cotangent, *, n_row, n_col
):
    nodes, width = features.shape
    sections, hub_rows = hub_ids.shape[0], hub_adj.shape[3]
    peers, slots, tile = recv_adj.shape[1], recv_adj.shape[2], recv_adj.shape[3]
    out_width = w_self.shape[1]
    tiles = nodes // tile
    first = min(peers * slots, tiles)
    group = 4
    send, count, dst = send_tile.swapaxes(1, 2)[0], recv_count, recv_dst.swapaxes(1, 2)[0]
    adj, weights, bias = hub_adj[0], recv_adj[0], bias.reshape(1, -1)
    params = pltpu.CompilerParams(vmem_limit_bytes=24 * 1024 * 1024)
    shape = jax.ShapeDtypeStruct
    sizes = dict(peers=peers, slots=slots, tile=tile)

    def cost(flops):
        return pl.CostEstimate(flops=flops, transcendentals=0, bytes_accessed=8 * nodes * width)

    def across(x, axis, size, d):
        return lax.ppermute(x, axis, [(i, i ^ d) for i in range(size)])

    order = exchange_order(n_col)
    pair = shape((slots, tile, width), BF16)
    own_hub, *picked = pl.pallas_call(
        functools.partial(pick_kernel, tile=tile),
        in_specs=[SMEM, HBM],
        out_specs=[VMEM] * (peers + 1),
        scratch_shapes=[pltpu.SemaphoreType.DMA((peers * slots + 1,))],
        out_shape=[shape((hub_rows, width), BF16)] + [pair] * peers,
        compiler_params=params,
        cost_estimate=pl.CostEstimate(flops=1000000000, transcendentals=0, bytes_accessed=0),
        name="pick",
    )(pltpu.with_memory_space_constraint(send, pltpu.HBM), pltpu.with_memory_space_constraint(features, pltpu.HBM))
    incoming = [picked[0]] + [None] * (peers - 1)
    for d in order:
        incoming[d] = across(picked[d], "col", n_col, d)
    same = jnp.stack([own_hub] + [across(own_hub, "row", n_row, d) for d in range(2, n_row, 2)])
    other = across(same, "row", n_row, 1)

    tile_at, place, own = pl.pallas_call(
        functools.partial(early_kernel, **sizes),
        in_specs=[SMEM] * 2 + [VMEM] * 3,
        out_specs=[SMEM] * 2 + [VMEM],
        out_shape=[shape((tiles,), jnp.int32)] * 2 + [shape((nodes, out_width), F32)],
        compiler_params=params,
        cost_estimate=pl.CostEstimate(flops=10000000000, transcendentals=0, bytes_accessed=0),
        name="early",
    )(count, dst, features, w_self, bias)

    def results(number):
        if not number:
            return []
        return [shape((number * tile, out_width), BF16)] * 2 + [shape((width, number * tile), BF16)]

    raw, deg, *others = pl.pallas_call(
        functools.partial(forward_kernel, tile=tile, chunk=256, group=group),
        in_specs=[SMEM] * 2 + [VMEM] * 6,
        out_specs=[VMEM] * (2 + len(results(tiles - first))),
        scratch_shapes=[pltpu.VMEM((sections * hub_rows, width), BF16)],
        out_shape=[shape((nodes, width), F32), shape((nodes, 128), F32)] + results(tiles - first),
        compiler_params=params,
        cost_estimate=cost(2 * sections * nodes * hub_rows * width),
        name="forward",
    )(tile_at, hub_ids, adj, same, other, own, cotangent, w_neigh)
    landed = pl.pallas_call(
        functools.partial(landed_kernel, group=group, **sizes),
        in_specs=[SMEM] * 4 + [VMEM] * (6 + peers),
        out_specs=[VMEM] * (3 + peers),
        scratch_shapes=[pltpu.VMEM((first * tile, n), t) for n, t in ((width, F32), (128, F32), (width, BF16))],
        out_shape=results(first) + [pair] * peers,
        compiler_params=params,
        name="landed",
    )(count, dst, tile_at, place, raw, deg, own, cotangent, weights, w_neigh, *incoming)
    outs, grads, turned = zip(*([landed[:3]] + ([others] if others else [])))
    going = landed[3:]
    returned = [going[0]] + [None] * (peers - 1)
    for d in order:
        returned[d] = across(going[d], "col", n_col, d)

    half = shape((n_row // 2, width, hub_rows), BF16)
    even, odd = pl.pallas_call(
        functools.partial(hub_backward_kernel, tile=tile),
        in_specs=[SMEM] * 2 + [VMEM] * (1 + len(turned)),
        out_specs=[VMEM] * 2,
        scratch_shapes=[pltpu.VMEM((n_row, width, hub_rows), F32)],
        out_shape=[half, half],
        compiler_params=params,
        cost_estimate=cost(2 * sections * nodes * hub_rows * width),
        name="hub_backward",
    )(tile_at, hub_ids, adj, *turned)
    came = across(odd, "row", n_row, 1)
    output, self_grad = pl.pallas_call(
        functools.partial(self_kernel, tile=tile),
        in_specs=[SMEM] + [VMEM] * (1 + 2 * len(outs)),
        out_specs=[HBM, VMEM],
        scratch_shapes=[pltpu.SemaphoreType.DMA((tiles,))],
        out_shape=[shape((nodes, out_width), BF16), shape((nodes, width), F32)],
        compiler_params=params,
        name="self",
    )(tile_at, w_self, *outs, *grads)
    block = shape((width, hub_rows), BF16)
    sums = pl.pallas_call(
        pair_add_kernel,
        out_shape=[block] * (n_row // 2),
        compiler_params=params,
        name="pair_add",
    )(even, came)
    hubs = [sums[0]] + [across(sums[d // 2], "row", n_row, d) for d in range(2, n_row, 2)]

    chunk = 2 * tile
    feature_grad, head = pl.pallas_call(
        functools.partial(tiles_kernel, chunk=chunk, **sizes),
        in_specs=[SMEM] + [VMEM] * (1 + peers),
        out_specs=[HBM, VMEM],
        scratch_shapes=[
            pltpu.VMEM((nodes, width), F32),
            pltpu.VMEM((nodes, width), BF16),
            pltpu.SemaphoreType.DMA(((nodes - hub_rows) // chunk,)),
        ],
        out_shape=[shape((nodes, width), BF16), shape((hub_rows, width), F32)],
        compiler_params=params,
        name="tiles_done",
    )(send, self_grad, *returned)
    feature_grad = pl.pallas_call(
        head_kernel,
        in_specs=[VMEM] * (1 + len(hubs)) + [HBM],
        out_specs=HBM,
        scratch_shapes=[pltpu.VMEM((hub_rows, width), BF16), pltpu.SemaphoreType.DMA],
        out_shape=shape((nodes, width), BF16),
        input_output_aliases={1 + len(hubs): 0},
        compiler_params=params,
        name="head",
    )(head, *hubs, feature_grad)
    return (output, feature_grad)


def exchange_order(n_col):
    return sorted(range(1, n_col), key=lambda d: (d != n_col // 2, d))


def solution(mesh):
    blocks = ("row", "col")
    placed = (
        P(blocks, None),
        P(),
        P(),
        P(),
        P(),
        P(blocks, None, None, None),
        P(blocks, None, None),
        P(blocks, None),
        P(blocks, None, None),
        P(blocks, None, None, None, None),
        P(blocks, None),
    )
    n_row, n_col = mesh.shape["row"], mesh.shape["col"]

    def body(*args):
        return shards(*args, n_row=n_row, n_col=n_col)

    return jax.shard_map(
        body, mesh=mesh, in_specs=placed, out_specs=(P(blocks, None), P(blocks, None)), check_vma=False
    )
```

```python
import functools

import jax
import jax.numpy as jnp
from jax import lax
from jax.experimental import pallas as pl
from jax.experimental.pallas import tpu as pltpu
from jax.sharding import PartitionSpec as P

F32 = jnp.float32
BF16 = jnp.bfloat16
BY_LAST = (((1,), (1,)), ((), ()))
BY_FIRST = (((0,), (0,)), ((), ()))
SMEM = pl.BlockSpec(memory_space=pltpu.SMEM)
ANY = pl.BlockSpec(memory_space=pl.ANY)
HBM = pl.BlockSpec(memory_space=pltpu.HBM)
VMEM = pl.BlockSpec(memory_space=pltpu.VMEM)


def rows_at(index, size):
    return pl.ds(pl.multiple_of(index * size, size), size)


def pick_kernel(send_in, feats_in, feats, hub, *rest):
    outs, (send, sems) = rest[:-2], rest[-2:]
    col = lax.axis_index("col")
    slots, tile, _ = outs[0].shape
    parts = sems.shape[0] - 1
    rows = feats.shape[0] // parts
    copies = [pltpu.make_async_copy(send_in, send, sems.at[parts])]
    for i in range(parts):
        at = pl.ds(i * rows, rows)
        copies.append(pltpu.make_async_copy(feats_in.at[at], feats.at[at], sems.at[i]))
    for copy in copies:
        copy.start()
    for copy in copies:
        copy.wait()
    hub[...] = feats[pl.ds(0, hub.shape[0]), :]
    for d, out in enumerate(outs):
        for k in range(slots):
            out[k] = feats[rows_at(send[k, col ^ d], tile), :]


def tile_order(count, dst, order, place, *, peers, slots, tiles):
    landed = jnp.int32(0)
    for p in range(peers):
        for k in range(slots):
            landed = landed | jnp.where(k < count[0, p], jnp.int32(1) << dst[k, p], 0)
    front, back = jnp.int32(0), jnp.int32(tiles - 1)
    for t in range(tiles):
        bit = (landed >> t) & 1
        at = jnp.where(bit == 1, front, back)
        order[at] = jnp.int32(t)
        place[t] = at
        front = front + bit
        back = back - (1 - bit)


def early_kernel(count, dst, feats, w_self, bias, order, place, own, *, peers, slots, tile):
    tile_order(count, dst, order, place, peers=peers, slots=slots, tiles=feats.shape[0] // tile)
    own[...] = jnp.dot(feats[...], w_self[...], preferred_element_type=F32) + bias[...]


def dense(raw, deg, own, cot, w_neigh):
    inverse = 1.0 / deg
    inverse = jnp.concatenate([inverse] * (raw.shape[1] // inverse.shape[1]), axis=1)
    agg = (raw * inverse).astype(BF16)
    pre = own + jnp.dot(agg, w_neigh[...], preferred_element_type=F32)
    sig = 0.5 * jnp.tanh(0.5 * pre) + 0.5
    out = (pre * sig).astype(BF16)
    grad = (cot.astype(F32) * sig * (1.0 + pre * (1.0 - sig))).astype(BF16)
    agg_grad = (lax.dot_general(grad, w_neigh[...], BY_LAST, preferred_element_type=F32) * inverse).astype(BF16)
    return out, grad, agg_grad


def forward_kernel(
    order, hub_ids, adj, same, other, own, cot, w_neigh, raw, deg, *rest, tile, chunk, group
):
    results, blocks = rest[:-1], rest[-1]
    row = lax.axis_index("row")
    sections, nodes, hub_rows = adj.shape
    for s in range(sections):
        away = hub_ids[s] ^ row
        at = pl.ds(s * hub_rows, hub_rows)

        @pl.when(away & 1 == 0)
        def _(away=away, at=at):
            blocks[at, :] = same[away >> 1]

        @pl.when(away & 1 == 1)
        def _(away=away, at=at):
            blocks[at, :] = other[away >> 1]

    tiles = nodes // tile
    for start in range(0, nodes, chunk):
        at = pl.ds(start, chunk)
        weights = jnp.concatenate([adj[s, at, :] for s in range(sections)], axis=1)
        raw[at, :] = jnp.dot(weights, blocks[...], preferred_element_type=F32)
        wide = weights.astype(F32)
        lanes = wide[:, 0:128]
        for c in range(128, wide.shape[1], 128):
            lanes = lanes + wide[:, c : c + 128]
        deg[at, :] = jnp.broadcast_to(1.0 + jnp.sum(lanes, axis=1, keepdims=True), (chunk, 128))
    if results:
        out, grad, turned = results
        first = tiles - out.shape[0] // tile
        for start in range(first, tiles, group):
            here = pl.ds((start - first) * tile, group * tile)
            there = [rows_at(order[i], tile) for i in range(start, start + group)]
            o, g, a = dense(
                *[jnp.concatenate([x[at, :] for at in there]) for x in (raw, deg, own, cot)], w_neigh
            )
            out[here, :] = o
            grad[here, :] = g
            turned[:, here] = a.T


def landed_kernel(count, dst, order, place, raw_in, deg_in, own, cot, adj, w_neigh, *rest, peers, slots, tile, group):
    inc = rest[:peers]
    out, grad, turned = rest[peers : peers + 3]
    back = rest[peers + 3 : 2 * peers + 3]
    raw, deg, agg_grad = rest[2 * peers + 3 :]
    col = lax.axis_index("col")
    first = raw.shape[0] // tile
    for i in range(first):
        at = rows_at(order[i], tile)
        raw[pl.ds(i * tile, tile), :] = raw_in[at, :]
        deg[pl.ds(i * tile, tile), :] = deg_in[at, :]
    parts = []
    for d in range(peers):
        p = col ^ d
        for k in range(slots):
            weights = adj[p, k]
            parts.append(
                (
                    k < count[0, p],
                    dst[k, p],
                    jnp.dot(weights, inc[d][k], preferred_element_type=F32),
                    jnp.sum(weights.astype(F32), axis=1, keepdims=True),
                )
            )
    for alive, target, part, lanes in parts:
        at = rows_at(jnp.where(alive, place[target], 0), tile)
        scale = jnp.where(alive, 1.0, 0.0).astype(F32)
        raw[at, :] += part * scale
        deg[at, :] += lanes * scale
    for start in range(0, first, group):
        here = pl.ds(start * tile, group * tile)
        there = [rows_at(order[i], tile) for i in range(start, start + group)]
        o, g, a = dense(
            raw[here, :],
            deg[here, :],
            jnp.concatenate([own[at, :] for at in there]),
            jnp.concatenate([cot[at, :] for at in there]),
            w_neigh,
        )
        out[here, :] = o
        grad[here, :] = g
        agg_grad[here, :] = a
        turned[:, here] = a.T
    for d in range(peers):
        p = col ^ d
        for k in range(slots):
            alive = k < count[0, p]
            at = rows_at(jnp.where(alive, place[dst[k, p]], 0), tile)
            part = lax.dot_general(adj[p, k], agg_grad[at, :], BY_FIRST, preferred_element_type=F32)
            back[d][k] = (part * jnp.where(alive, 1.0, 0.0).astype(F32)).astype(BF16)


def hub_backward_kernel(order, hub_ids, adj, *rest, tile):
    pieces, (even, odd, acc) = rest[:-3], rest[-3:]
    row = lax.axis_index("row")
    sections, nodes, _ = adj.shape
    there = [rows_at(order[i], tile) for i in range(nodes // tile)]
    acc[...] = jnp.zeros_like(acc)
    for s in range(sections):
        turned = jnp.concatenate([piece[...] for piece in pieces], axis=1)
        weights = jnp.concatenate([adj[s, at, :] for at in there])
        acc[hub_ids[s] ^ row] += jnp.dot(turned, weights, preferred_element_type=F32)
    for e in range(even.shape[0]):
        even[e] = acc[2 * e].astype(BF16)
        odd[e] = acc[2 * e + 1].astype(BF16)


def self_kernel(order, w_self, *rest, tile):
    pieces, (out, self_grad, sems) = rest[:-3], rest[-3:]
    copies = []
    i = 0
    for outs, grads in zip(pieces[: len(pieces) // 2], pieces[len(pieces) // 2 :]):
        for j in range(outs.shape[0] // tile):
            copies.append(
                pltpu.make_async_copy(outs.at[pl.ds(j * tile, tile)], out.at[rows_at(order[i], tile)], sems.at[i])
            )
            copies[-1].start()
            i += 1
    i = 0
    for grads in pieces[len(pieces) // 2 :]:
        through = lax.dot_general(grads[...], w_self[...], BY_LAST, preferred_element_type=F32)
        for j in range(grads.shape[0] // tile):
            self_grad[rows_at(order[i], tile), :] = through[j * tile : (j + 1) * tile]
            i += 1
    for copy in copies:
        copy.wait()


def pair_add_kernel(even, came, *outs):
    for e, out in enumerate(outs):
        out[...] = (even[e].astype(F32) + came[e].astype(F32)).astype(BF16)


def tiles_kernel(send, self_grad, *rest, peers, slots, tile, chunk):
    back, (out, head, total, done, sems) = rest[:peers], rest[peers:]
    col = lax.axis_index("col")
    total[...] = self_grad[...]
    for d in range(peers):
        for k in range(slots):
            total[rows_at(send[k, col ^ d], tile), :] += back[d][k].astype(F32)
    head[...] = total[pl.ds(0, head.shape[0]), :]
    copies = []
    for i, start in enumerate(range(head.shape[0], total.shape[0], chunk)):
        at = pl.ds(start, chunk)
        done[at, :] = total[at, :].astype(BF16)
        copies.append(pltpu.make_async_copy(done.at[at], out.at[at], sems.at[i]))
        copies[-1].start()
    for copy in copies:
        copy.wait()


def head_kernel(head, *rest):
    hub, (_, out, done, sem) = rest[:-4], rest[-4:]
    come = hub[0][...].astype(F32)
    for h in hub[1:]:
        come = come + h[...].astype(F32)
    done[...] = (head[...] + come.T).astype(BF16)
    copy = pltpu.make_async_copy(done, out.at[pl.ds(0, done.shape[0])], sem)
    copy.start()
    copy.wait()


def shards(
    features, w_self, w_neigh, bias, hub_ids, hub_adj, send_tile, recv_count, recv_dst, recv_adj, cotangent, *, n_row, n_col
):
    nodes, width = features.shape
    sections, hub_rows = hub_ids.shape[0], hub_adj.shape[3]
    peers, slots, tile = recv_adj.shape[1], recv_adj.shape[2], recv_adj.shape[3]
    out_width = w_self.shape[1]
    tiles = nodes // tile
    first = min(peers * slots, tiles)
    group = 4
    send, count, dst = send_tile.swapaxes(1, 2)[0], recv_count, recv_dst.swapaxes(1, 2)[0]
    adj, weights, bias = hub_adj[0], recv_adj[0], bias.reshape(1, -1)
    params = pltpu.CompilerParams(vmem_limit_bytes=24 * 1024 * 1024)
    shape = jax.ShapeDtypeStruct
    sizes = dict(peers=peers, slots=slots, tile=tile)

    def cost(flops):
        return pl.CostEstimate(flops=flops, transcendentals=0, bytes_accessed=8 * nodes * width)

    def across(x, axis, size, d):
        return lax.ppermute(x, axis, [(i, i ^ d) for i in range(size)])

    order = exchange_order(n_col)
    pair = shape((slots, tile, width), BF16)
    feats, own_hub, *picked = pl.pallas_call(
        pick_kernel,
        in_specs=[HBM, HBM],
        out_specs=[VMEM] * (peers + 2),
        scratch_shapes=[pltpu.SMEM(send.shape, jnp.int32), pltpu.SemaphoreType.DMA((5,))],
        out_shape=[shape((nodes, width), BF16), shape((hub_rows, width), BF16)] + [pair] * peers,
        compiler_params=params,
        cost_estimate=pl.CostEstimate(flops=1000000000, transcendentals=0, bytes_accessed=0),
        name="pick",
    )(pltpu.with_memory_space_constraint(send, pltpu.HBM), pltpu.with_memory_space_constraint(features, pltpu.HBM))
    incoming = [picked[0]] + [None] * (peers - 1)
    for d in order:
        incoming[d] = across(picked[d], "col", n_col, d)
    same = jnp.stack([own_hub] + [across(own_hub, "row", n_row, d) for d in range(2, n_row, 2)])
    other = across(same, "row", n_row, 1)

    tile_at, place, own = pl.pallas_call(
        functools.partial(early_kernel, **sizes),
        in_specs=[SMEM] * 2 + [VMEM] * 3,
        out_specs=[SMEM] * 2 + [VMEM],
        out_shape=[shape((tiles,), jnp.int32)] * 2 + [shape((nodes, out_width), F32)],
        compiler_params=params,
        cost_estimate=pl.CostEstimate(flops=10000000000, transcendentals=0, bytes_accessed=0),
        name="early",
    )(count, dst, feats, w_self, bias)

    def results(number):
        if not number:
            return []
        return [shape((number * tile, out_width), BF16)] * 2 + [shape((width, number * tile), BF16)]

    raw, deg, *others = pl.pallas_call(
        functools.partial(forward_kernel, tile=tile, chunk=256, group=group),
        in_specs=[SMEM] * 2 + [VMEM] * 6,
        out_specs=[VMEM] * (2 + len(results(tiles - first))),
        scratch_shapes=[pltpu.VMEM((sections * hub_rows, width), BF16)],
        out_shape=[shape((nodes, width), F32), shape((nodes, 128), F32)] + results(tiles - first),
        compiler_params=params,
        cost_estimate=cost(2 * sections * nodes * hub_rows * width),
        name="forward",
    )(tile_at, hub_ids, adj, same, other, own, cotangent, w_neigh)
    landed = pl.pallas_call(
        functools.partial(landed_kernel, group=group, **sizes),
        in_specs=[SMEM] * 4 + [VMEM] * (6 + peers),
        out_specs=[VMEM] * (3 + peers),
        scratch_shapes=[pltpu.VMEM((first * tile, n), t) for n, t in ((width, F32), (128, F32), (width, BF16))],
        out_shape=results(first) + [pair] * peers,
        compiler_params=params,
        name="landed",
    )(count, dst, tile_at, place, raw, deg, own, cotangent, weights, w_neigh, *incoming)
    outs, grads, turned = zip(*([landed[:3]] + ([others] if others else [])))
    going = landed[3:]
    returned = [going[0]] + [None] * (peers - 1)
    for d in order:
        returned[d] = across(going[d], "col", n_col, d)

    half = shape((n_row // 2, width, hub_rows), BF16)
    even, odd = pl.pallas_call(
        functools.partial(hub_backward_kernel, tile=tile),
        in_specs=[SMEM] * 2 + [VMEM] * (1 + len(turned)),
        out_specs=[VMEM] * 2,
        scratch_shapes=[pltpu.VMEM((n_row, width, hub_rows), F32)],
        out_shape=[half, half],
        compiler_params=params,
        cost_estimate=cost(2 * sections * nodes * hub_rows * width),
        name="hub_backward",
    )(tile_at, hub_ids, adj, *turned)
    came = across(odd, "row", n_row, 1)
    output, self_grad = pl.pallas_call(
        functools.partial(self_kernel, tile=tile),
        in_specs=[SMEM] + [VMEM] * (1 + 2 * len(outs)),
        out_specs=[HBM, VMEM],
        scratch_shapes=[pltpu.SemaphoreType.DMA((tiles,))],
        out_shape=[shape((nodes, out_width), BF16), shape((nodes, width), F32)],
        compiler_params=params,
        name="self",
    )(tile_at, w_self, *outs, *grads)
    block = shape((width, hub_rows), BF16)
    sums = pl.pallas_call(
        pair_add_kernel,
        out_shape=[block] * (n_row // 2),
        compiler_params=params,
        name="pair_add",
    )(even, came)
    hubs = [sums[0]] + [across(sums[d // 2], "row", n_row, d) for d in range(2, n_row, 2)]

    chunk = 2 * tile
    feature_grad, head = pl.pallas_call(
        functools.partial(tiles_kernel, chunk=chunk, **sizes),
        in_specs=[SMEM] + [VMEM] * (1 + peers),
        out_specs=[HBM, VMEM],
        scratch_shapes=[
            pltpu.VMEM((nodes, width), F32),
            pltpu.VMEM((nodes, width), BF16),
            pltpu.SemaphoreType.DMA(((nodes - hub_rows) // chunk,)),
        ],
        out_shape=[shape((nodes, width), BF16), shape((hub_rows, width), F32)],
        compiler_params=params,
        name="tiles_done",
    )(send, self_grad, *returned)
    feature_grad = pl.pallas_call(
        head_kernel,
        in_specs=[VMEM] * (1 + len(hubs)) + [HBM],
        out_specs=HBM,
        scratch_shapes=[pltpu.VMEM((hub_rows, width), BF16), pltpu.SemaphoreType.DMA],
        out_shape=shape((nodes, width), BF16),
        input_output_aliases={1 + len(hubs): 0},
        compiler_params=params,
        name="head",
    )(head, *hubs, feature_grad)
    return (output, feature_grad)


def exchange_order(n_col):
    return sorted(range(1, n_col), key=lambda d: (d != n_col // 2, d))


def solution(mesh):
    blocks = ("row", "col")
    placed = (
        P(blocks, None),
        P(),
        P(),
        P(),
        P(),
        P(blocks, None, None, None),
        P(blocks, None, None),
        P(blocks, None),
        P(blocks, None, None),
        P(blocks, None, None, None, None),
        P(blocks, None),
    )
    n_row, n_col = mesh.shape["row"], mesh.shape["col"]

    def body(*args):
        return shards(*args, n_row=n_row, n_col=n_col)

    return jax.shard_map(
        body, mesh=mesh, in_specs=placed, out_specs=(P(blocks, None), P(blocks, None)), check_vma=False
    )
```

```python
import functools

import jax
import jax.numpy as jnp
from jax import lax
from jax.experimental import pallas as pl
from jax.experimental.pallas import tpu as pltpu
from jax.sharding import PartitionSpec as P

F32 = jnp.float32
BF16 = jnp.bfloat16
BY_LAST = (((1,), (1,)), ((), ()))
BY_FIRST = (((0,), (0,)), ((), ()))
SMEM = pl.BlockSpec(memory_space=pltpu.SMEM)
ANY = pl.BlockSpec(memory_space=pl.ANY)
HBM = pl.BlockSpec(memory_space=pltpu.HBM)
VMEM = pl.BlockSpec(memory_space=pltpu.VMEM)


def rows_at(index, size):
    return pl.ds(pl.multiple_of(index * size, size), size)


def pick_kernel(send_in, feats_in, feats, hub, *rest):
    outs, (send, sems) = rest[:-2], rest[-2:]
    col = lax.axis_index("col")
    slots, tile, _ = outs[0].shape
    parts = sems.shape[0] - 1
    rows = feats.shape[0] // parts
    copies = [pltpu.make_async_copy(send_in, send, sems.at[parts])]
    for i in range(parts):
        at = pl.ds(i * rows, rows)
        copies.append(pltpu.make_async_copy(feats_in.at[at], feats.at[at], sems.at[i]))
    for copy in copies:
        copy.start()
    for copy in copies:
        copy.wait()
    hub[...] = feats[pl.ds(0, hub.shape[0]), :]
    for d, out in enumerate(outs):
        for k in range(slots):
            out[k] = feats[rows_at(send[k, col ^ d], tile), :]


def tile_order(count, dst, order, place, *, peers, slots, tiles):
    landed = jnp.int32(0)
    for p in range(peers):
        for k in range(slots):
            landed = landed | jnp.where(k < count[0, p], jnp.int32(1) << dst[k, p], 0)
    front, back = jnp.int32(0), jnp.int32(tiles - 1)
    for t in range(tiles):
        bit = (landed >> t) & 1
        at = jnp.where(bit == 1, front, back)
        order[at] = jnp.int32(t)
        place[t] = at
        front = front + bit
        back = back - (1 - bit)


def early_kernel(feats, w_self, bias, own):
    own[...] = jnp.dot(feats[...], w_self[...], preferred_element_type=F32) + bias[...]


def degree_kernel(adj, deg, *, chunk):
    sections, nodes, hub_rows = adj.shape
    for start in range(0, nodes, chunk):
        at = pl.ds(start, chunk)
        lanes = jnp.zeros((chunk, 128), F32)
        for s in range(sections):
            for c in range(0, hub_rows, 128):
                lanes = lanes + adj[s, at, c : c + 128].astype(F32)
        deg[at, :] = jnp.broadcast_to(1.0 + jnp.sum(lanes, axis=1, keepdims=True), (chunk, 128))


def dense(raw, deg, own, cot, w_neigh):
    inverse = 1.0 / deg
    inverse = jnp.concatenate([inverse] * (raw.shape[1] // inverse.shape[1]), axis=1)
    agg = (raw * inverse).astype(BF16)
    pre = own + jnp.dot(agg, w_neigh[...], preferred_element_type=F32)
    sig = 0.5 * jnp.tanh(0.5 * pre) + 0.5
    silu = pre * sig
    out = silu.astype(BF16)
    grad = (cot.astype(F32) * (sig + silu * (1.0 - sig))).astype(BF16)
    agg_grad = (lax.dot_general(grad, w_neigh[...], BY_LAST, preferred_element_type=F32) * inverse).astype(BF16)
    return out, grad, agg_grad


def forward_kernel(
    order, hub_ids, adj, same, other, deg, own, cot, w_neigh, raw, *rest, tile, chunk, group
):
    results, blocks = rest[:-1], rest[-1]
    row = lax.axis_index("row")
    sections, nodes, hub_rows = adj.shape
    for s in range(sections):
        away = hub_ids[s] ^ row
        at = pl.ds(s * hub_rows, hub_rows)

        @pl.when(away & 1 == 0)
        def _(away=away, at=at):
            blocks[at, :] = same[away >> 1]

        @pl.when(away & 1 == 1)
        def _(away=away, at=at):
            blocks[at, :] = other[away >> 1]

    tiles = nodes // tile
    for start in range(0, nodes, chunk):
        at = pl.ds(start, chunk)
        weights = jnp.concatenate([adj[s, at, :] for s in range(sections)], axis=1)
        raw[at, :] = jnp.dot(weights, blocks[...], preferred_element_type=F32)
    if results:
        out, grad, turned = results
        first = tiles - out.shape[0] // tile
        for start in range(first, tiles, group):
            here = pl.ds((start - first) * tile, group * tile)
            there = [rows_at(order[i], tile) for i in range(start, start + group)]
            o, g, a = dense(
                *[jnp.concatenate([x[at, :] for at in there]) for x in (raw, deg, own, cot)], w_neigh
            )
            out[here, :] = o
            grad[here, :] = g
            turned[:, here] = a.T


def landed_kernel(count, dst, order, place, raw_in, deg_in, own, cot, adj, w_neigh, *rest, peers, slots, tile, group):
    inc = rest[:peers]
    out, grad, turned = rest[peers : peers + 3]
    back = rest[peers + 3 : 2 * peers + 3]
    raw, deg, agg_grad = rest[2 * peers + 3 :]
    col = lax.axis_index("col")
    first = raw.shape[0] // tile
    for i in range(first):
        at = rows_at(order[i], tile)
        raw[pl.ds(i * tile, tile), :] = raw_in[at, :]
        deg[pl.ds(i * tile, tile), :] = deg_in[at, :]
    parts = []
    for d in range(peers):
        p = col ^ d
        for k in range(slots):
            weights = adj[p, k]
            parts.append(
                (
                    k < count[0, p],
                    dst[k, p],
                    jnp.dot(weights, inc[d][k], preferred_element_type=F32),
                    jnp.sum(weights.astype(F32), axis=1, keepdims=True),
                )
            )
    for alive, target, part, lanes in parts:
        at = rows_at(jnp.where(alive, place[target], 0), tile)
        scale = jnp.where(alive, 1.0, 0.0).astype(F32)
        raw[at, :] += part * scale
        deg[at, :] += lanes * scale
    for start in range(0, first, group):
        here = pl.ds(start * tile, group * tile)
        there = [rows_at(order[i], tile) for i in range(start, start + group)]
        o, g, a = dense(
            raw[here, :],
            deg[here, :],
            jnp.concatenate([own[at, :] for at in there]),
            jnp.concatenate([cot[at, :] for at in there]),
            w_neigh,
        )
        out[here, :] = o
        grad[here, :] = g
        agg_grad[here, :] = a
        turned[:, here] = a.T
    for d in range(peers):
        p = col ^ d
        for k in range(slots):
            alive = k < count[0, p]
            at = rows_at(jnp.where(alive, place[dst[k, p]], 0), tile)
            part = lax.dot_general(adj[p, k], agg_grad[at, :], BY_FIRST, preferred_element_type=F32)
            back[d][k] = (part * jnp.where(alive, 1.0, 0.0).astype(F32)).astype(BF16)


def hub_backward_kernel(order, hub_ids, adj, *rest, tile):
    pieces, (even, odd, acc) = rest[:-3], rest[-3:]
    row = lax.axis_index("row")
    sections, nodes, _ = adj.shape
    there = [rows_at(order[i], tile) for i in range(nodes // tile)]
    acc[...] = jnp.zeros_like(acc)
    for s in range(sections):
        turned = jnp.concatenate([piece[...] for piece in pieces], axis=1)
        weights = jnp.concatenate([adj[s, at, :] for at in there])
        acc[hub_ids[s] ^ row] += jnp.dot(turned, weights, preferred_element_type=F32)
    for e in range(even.shape[0]):
        even[e] = acc[2 * e].astype(BF16)
        odd[e] = acc[2 * e + 1].astype(BF16)


def self_kernel(order, w_self, *rest, tile):
    pieces, (out, total, self_grad, narrow, sems) = rest[:-5], rest[-5:]
    copies = []
    i = 0
    for outs, grads in zip(pieces[: len(pieces) // 2], pieces[len(pieces) // 2 :]):
        for j in range(outs.shape[0] // tile):
            copies.append(
                pltpu.make_async_copy(outs.at[pl.ds(j * tile, tile)], out.at[rows_at(order[i], tile)], sems.at[i])
            )
            copies[-1].start()
            i += 1
    i = 0
    for grads in pieces[len(pieces) // 2 :]:
        through = lax.dot_general(grads[...], w_self[...], BY_LAST, preferred_element_type=F32)
        for j in range(grads.shape[0] // tile):
            at = rows_at(order[i], tile)
            self_grad[at, :] = through[j * tile : (j + 1) * tile]
            narrow[at, :] = through[j * tile : (j + 1) * tile].astype(BF16)
            i += 1
    parts = sems.shape[0] - len(copies)
    rows = narrow.shape[0] // parts
    for i in range(parts):
        at = pl.ds(i * rows, rows)
        copies.append(pltpu.make_async_copy(narrow.at[at], total.at[at], sems.at[len(copies)]))
        copies[-1].start()
    for copy in copies:
        copy.wait()


def pair_add_kernel(even, came, *outs):
    for e, out in enumerate(outs):
        out[...] = (even[e].astype(F32) + came[e].astype(F32)).astype(BF16)


def tiles_kernel(send, self_grad, *rest, peers, slots, tile):
    back, (_, out, head, total, done, sems) = rest[:peers], rest[peers:]
    col = lax.axis_index("col")
    targets = [send[k, col ^ d] for d in range(peers) for k in range(slots)]
    spots = [rows_at(target, tile) for target in targets]
    top = pl.ds(0, head.shape[0])
    total[top, :] = self_grad[top, :]
    for at in spots:
        total[at, :] = self_grad[at, :]
    for i, at in enumerate(spots):
        total[at, :] += back[i // slots][i % slots].astype(F32)
    copies = []
    for i, at in enumerate(spots):
        fresh = targets[i] * tile >= head.shape[0]
        for other in targets[:i]:
            fresh = fresh & (other != targets[i])
        done[i] = total[at, :].astype(BF16)
        copy = pltpu.make_async_copy(done.at[i], out.at[at], sems.at[i])
        pl.when(fresh)(copy.start)
        copies.append((fresh, copy))
    head[...] = total[top, :]
    for fresh, copy in copies:
        pl.when(fresh)(copy.wait)


def head_kernel(head, *rest):
    hub, (_, out, done, sem) = rest[:-4], rest[-4:]
    come = hub[0][...].astype(F32)
    for h in hub[1:]:
        come = come + h[...].astype(F32)
    done[...] = (head[...] + come.T).astype(BF16)
    copy = pltpu.make_async_copy(done, out.at[pl.ds(0, done.shape[0])], sem)
    copy.start()
    copy.wait()


def shards(
    features, w_self, w_neigh, bias, hub_ids, hub_adj, send_tile, recv_count, recv_dst, recv_adj, cotangent, *, n_row, n_col
):
    nodes, width = features.shape
    sections, hub_rows = hub_ids.shape[0], hub_adj.shape[3]
    peers, slots, tile = recv_adj.shape[1], recv_adj.shape[2], recv_adj.shape[3]
    out_width = w_self.shape[1]
    tiles = nodes // tile
    first = min(peers * slots, tiles)
    group = 4
    send, count, dst = send_tile.swapaxes(1, 2)[0], recv_count, recv_dst.swapaxes(1, 2)[0]
    adj, weights, bias = hub_adj[0], recv_adj[0], bias.reshape(1, -1)
    params = pltpu.CompilerParams(vmem_limit_bytes=24 * 1024 * 1024)
    shape = jax.ShapeDtypeStruct
    sizes = dict(peers=peers, slots=slots, tile=tile)

    def cost(flops):
        return pl.CostEstimate(flops=flops, transcendentals=0, bytes_accessed=8 * nodes * width)

    def across(x, axis, size, d):
        return lax.ppermute(x, axis, [(i, i ^ d) for i in range(size)])

    order = exchange_order(n_col)
    pair = shape((slots, tile, width), BF16)
    feats, own_hub, *picked = pl.pallas_call(
        pick_kernel,
        in_specs=[HBM, HBM],
        out_specs=[VMEM] * (peers + 2),
        scratch_shapes=[pltpu.SMEM(send.shape, jnp.int32), pltpu.SemaphoreType.DMA((5,))],
        out_shape=[shape((nodes, width), BF16), shape((hub_rows, width), BF16)] + [pair] * peers,
        compiler_params=params,
        cost_estimate=pl.CostEstimate(flops=1000000000, transcendentals=0, bytes_accessed=0),
        name="pick",
    )(pltpu.with_memory_space_constraint(send, pltpu.HBM), pltpu.with_memory_space_constraint(features, pltpu.HBM))
    incoming = [picked[0]] + [None] * (peers - 1)
    for d in order:
        incoming[d] = across(picked[d], "col", n_col, d)
    same = jnp.stack([own_hub] + [across(own_hub, "row", n_row, d) for d in range(2, n_row, 2)])
    other = across(same, "row", n_row, 1)

    own = pl.pallas_call(
        early_kernel,
        in_specs=[VMEM] * 3,
        out_specs=VMEM,
        out_shape=shape((nodes, out_width), F32),
        compiler_params=params,
        cost_estimate=pl.CostEstimate(flops=1000000000, transcendentals=0, bytes_accessed=0),
        name="early",
    )(feats, w_self, bias)
    tile_at, place = pl.pallas_call(
        functools.partial(tile_order, peers=peers, slots=slots, tiles=tiles),
        in_specs=[SMEM] * 2,
        out_specs=[SMEM] * 2,
        out_shape=[shape((tiles,), jnp.int32)] * 2,
        compiler_params=params,
        cost_estimate=pl.CostEstimate(flops=10000000000, transcendentals=0, bytes_accessed=0),
        name="tables",
    )(count, dst)

    def results(number):
        if not number:
            return []
        return [shape((number * tile, out_width), BF16)] * 2 + [shape((width, number * tile), BF16)]

    deg = pl.pallas_call(
        functools.partial(degree_kernel, chunk=256),
        in_specs=[VMEM],
        out_specs=VMEM,
        out_shape=shape((nodes, 128), F32),
        compiler_params=params,
        name="degree",
    )(adj)
    raw, *others = pl.pallas_call(
        functools.partial(forward_kernel, tile=tile, chunk=256, group=group),
        in_specs=[SMEM] * 2 + [VMEM] * 7,
        out_specs=[VMEM] * (1 + len(results(tiles - first))),
        scratch_shapes=[pltpu.VMEM((sections * hub_rows, width), BF16)],
        out_shape=[shape((nodes, width), F32)] + results(tiles - first),
        compiler_params=params,
        cost_estimate=cost(2 * sections * nodes * hub_rows * width),
        name="forward",
    )(tile_at, hub_ids, adj, same, other, deg, own, cotangent, w_neigh)
    landed = pl.pallas_call(
        functools.partial(landed_kernel, group=group, **sizes),
        in_specs=[SMEM] * 4 + [VMEM] * (6 + peers),
        out_specs=[VMEM] * (3 + peers),
        scratch_shapes=[pltpu.VMEM((first * tile, n), t) for n, t in ((width, F32), (128, F32), (width, BF16))],
        out_shape=results(first) + [pair] * peers,
        compiler_params=params,
        name="landed",
    )(count, dst, tile_at, place, raw, deg, own, cotangent, weights, w_neigh, *incoming)
    outs, grads, turned = zip(*([landed[:3]] + ([others] if others else [])))
    going = landed[3:]
    returned = [going[0]] + [None] * (peers - 1)
    for d in order:
        returned[d] = across(going[d], "col", n_col, d)

    half = shape((n_row // 2, width, hub_rows), BF16)
    even, odd = pl.pallas_call(
        functools.partial(hub_backward_kernel, tile=tile),
        in_specs=[SMEM] * 2 + [VMEM] * (1 + len(turned)),
        out_specs=[VMEM] * 2,
        scratch_shapes=[pltpu.VMEM((n_row, width, hub_rows), F32)],
        out_shape=[half, half],
        compiler_params=params,
        cost_estimate=cost(2 * sections * nodes * hub_rows * width),
        name="hub_backward",
    )(tile_at, hub_ids, adj, *turned)
    came = across(odd, "row", n_row, 1)
    output, feature_grad, self_grad = pl.pallas_call(
        functools.partial(self_kernel, tile=tile),
        in_specs=[SMEM] + [VMEM] * (1 + 2 * len(outs)),
        out_specs=[HBM, HBM, VMEM],
        scratch_shapes=[pltpu.VMEM((nodes, width), BF16), pltpu.SemaphoreType.DMA((tiles + 4,))],
        out_shape=[shape((nodes, out_width), BF16), shape((nodes, width), BF16), shape((nodes, width), F32)],
        compiler_params=params,
        name="self",
    )(tile_at, w_self, *outs, *grads)
    block = shape((width, hub_rows), BF16)
    sums = pl.pallas_call(
        pair_add_kernel,
        out_shape=[block] * (n_row // 2),
        compiler_params=params,
        name="pair_add",
    )(even, came)
    hubs = [sums[0]] + [across(sums[d // 2], "row", n_row, d) for d in range(2, n_row, 2)]

    whole = shape((nodes, width), BF16)
    feature_grad, head = pl.pallas_call(
        functools.partial(tiles_kernel, **sizes),
        in_specs=[SMEM] + [VMEM] * (1 + peers) + [HBM],
        out_specs=[HBM, VMEM],
        scratch_shapes=[
            pltpu.VMEM((nodes, width), F32),
            pltpu.VMEM((peers * slots, tile, width), BF16),
            pltpu.SemaphoreType.DMA((peers * slots,)),
        ],
        out_shape=[whole, shape((hub_rows, width), F32)],
        input_output_aliases={2 + peers: 0},
        compiler_params=params,
        name="tiles_done",
    )(send, self_grad, *returned, feature_grad)
    feature_grad = pl.pallas_call(
        head_kernel,
        in_specs=[VMEM] * (1 + len(hubs)) + [HBM],
        out_specs=HBM,
        scratch_shapes=[pltpu.VMEM((hub_rows, width), BF16), pltpu.SemaphoreType.DMA],
        out_shape=whole,
        input_output_aliases={1 + len(hubs): 0},
        compiler_params=params,
        name="head",
    )(head, *hubs, feature_grad)
    return (output, feature_grad)


def exchange_order(n_col):
    return sorted(range(1, n_col), key=lambda d: (d != n_col // 2, d))


def solution(mesh):
    blocks = ("row", "col")
    placed = (
        P(blocks, None),
        P(),
        P(),
        P(),
        P(),
        P(blocks, None, None, None),
        P(blocks, None, None),
        P(blocks, None),
        P(blocks, None, None),
        P(blocks, None, None, None, None),
        P(blocks, None),
    )
    n_row, n_col = mesh.shape["row"], mesh.shape["col"]

    def body(*args):
        return shards(*args, n_row=n_row, n_col=n_col)

    return jax.shard_map(
        body, mesh=mesh, in_specs=placed, out_specs=(P(blocks, None), P(blocks, None)), check_vma=False
    )
```

```python
import functools

import jax
import jax.numpy as jnp
from jax import lax
from jax.experimental import pallas as pl
from jax.experimental.pallas import tpu as pltpu
from jax.sharding import PartitionSpec as P

F32 = jnp.float32
BF16 = jnp.bfloat16
BY_LAST = (((1,), (1,)), ((), ()))
BY_FIRST = (((0,), (0,)), ((), ()))
SMEM = pl.BlockSpec(memory_space=pltpu.SMEM)
ANY = pl.BlockSpec(memory_space=pl.ANY)
HBM = pl.BlockSpec(memory_space=pltpu.HBM)
VMEM = pl.BlockSpec(memory_space=pltpu.VMEM)


def rows_at(index, size):
    return pl.ds(pl.multiple_of(index * size, size), size)


def pick_kernel(send_in, feats_in, feats, hub, *rest):
    outs, (send, sems) = rest[:-2], rest[-2:]
    col = lax.axis_index("col")
    slots, tile, _ = outs[0].shape
    parts = sems.shape[0] - 1
    rows = feats.shape[0] // parts
    copies = [pltpu.make_async_copy(send_in, send, sems.at[parts])]
    for i in range(parts):
        at = pl.ds(i * rows, rows)
        copies.append(pltpu.make_async_copy(feats_in.at[at], feats.at[at], sems.at[i]))
    for copy in copies:
        copy.start()
    for copy in copies:
        copy.wait()
    hub[...] = feats[pl.ds(0, hub.shape[0]), :]
    for d, out in enumerate(outs):
        for k in range(slots):
            out[k] = feats[rows_at(send[k, col ^ d], tile), :]


def tile_order(count, dst, order, place, *, peers, slots, tiles):
    landed = jnp.int32(0)
    for p in range(peers):
        for k in range(slots):
            landed = landed | jnp.where(k < count[0, p], jnp.int32(1) << dst[k, p], 0)
    front, back = jnp.int32(0), jnp.int32(tiles - 1)
    for t in range(tiles):
        bit = (landed >> t) & 1
        at = jnp.where(bit == 1, front, back)
        order[at] = jnp.int32(t)
        place[t] = at
        front = front + bit
        back = back - (1 - bit)


def early_kernel(feats, w_self, bias, own):
    own[...] = jnp.dot(feats[...], w_self[...], preferred_element_type=F32) + bias[...]


def degree_kernel(adj, deg, *, chunk):
    sections, nodes, hub_rows = adj.shape
    for start in range(0, nodes, chunk):
        at = pl.ds(start, chunk)
        lanes = jnp.zeros((chunk, 128), F32)
        for s in range(sections):
            for c in range(0, hub_rows, 128):
                lanes = lanes + adj[s, at, c : c + 128].astype(F32)
        deg[at, :] = jnp.broadcast_to(1.0 + jnp.sum(lanes, axis=1, keepdims=True), (chunk, 128))


def dense(raw, deg, own, cot, w_neigh):
    inverse = 1.0 / deg
    inverse = jnp.concatenate([inverse] * (raw.shape[1] // inverse.shape[1]), axis=1)
    agg = (raw * inverse).astype(BF16)
    pre = own + jnp.dot(agg, w_neigh[...], preferred_element_type=F32)
    sig = 0.5 * jnp.tanh(0.5 * pre) + 0.5
    silu = pre * sig
    out = silu.astype(BF16)
    grad = (cot.astype(F32) * (sig + silu * (1.0 - sig))).astype(BF16)
    agg_grad = (lax.dot_general(grad, w_neigh[...], BY_LAST, preferred_element_type=F32) * inverse).astype(BF16)
    return out, grad, agg_grad


def forward_kernel(
    order, hub_ids, adj, same, other, deg, own, cot, w_neigh, raw, *rest, tile, chunk, group
):
    results, blocks = rest[:-1], rest[-1]
    if results:
        results, blocks = results[:-1] + rest[-1:], results[-1]
    row = lax.axis_index("row")
    sections, nodes, hub_rows = adj.shape
    for s in range(sections):
        away = hub_ids[s] ^ row
        at = pl.ds(s * hub_rows, hub_rows)

        @pl.when(away & 1 == 0)
        def _(away=away, at=at):
            blocks[at, :] = same[away >> 1]

        @pl.when(away & 1 == 1)
        def _(away=away, at=at):
            blocks[at, :] = other[away >> 1]

    tiles = nodes // tile
    for start in range(0, nodes, chunk):
        at = pl.ds(start, chunk)
        weights = jnp.concatenate([adj[s, at, :] for s in range(sections)], axis=1)
        raw[at, :] = jnp.dot(weights, blocks[...], preferred_element_type=F32)
    if results:
        out, grad, acc, turned = results
        first = tiles - out.shape[0] // tile
        for start in range(first, tiles, group):
            here = pl.ds((start - first) * tile, group * tile)
            there = [rows_at(order[i], tile) for i in range(start, start + group)]
            o, g, a = dense(
                *[jnp.concatenate([x[at, :] for at in there]) for x in (raw, deg, own, cot)], w_neigh
            )
            out[here, :] = o
            grad[here, :] = g
            turned[:, here] = a.T
        acc[...] = jnp.zeros_like(acc)
        for s in range(sections):
            weights = jnp.concatenate([adj[s, rows_at(order[i], tile), :] for i in range(first, tiles)])
            acc[hub_ids[s] ^ row] += jnp.dot(turned[...], weights, preferred_element_type=F32)


def landed_kernel(count, dst, order, place, raw_in, deg_in, own, cot, adj, w_neigh, *rest, peers, slots, tile, group):
    inc = rest[:peers]
    out, grad, turned = rest[peers : peers + 3]
    back = rest[peers + 3 : 2 * peers + 3]
    raw, deg, agg_grad = rest[2 * peers + 3 :]
    col = lax.axis_index("col")
    first = raw.shape[0] // tile
    for i in range(first):
        at = rows_at(order[i], tile)
        raw[pl.ds(i * tile, tile), :] = raw_in[at, :]
        deg[pl.ds(i * tile, tile), :] = deg_in[at, :]
    parts = []
    for d in range(peers):
        p = col ^ d
        for k in range(slots):
            weights = adj[p, k]
            parts.append(
                (
                    k < count[0, p],
                    dst[k, p],
                    jnp.dot(weights, inc[d][k], preferred_element_type=F32),
                    jnp.sum(weights.astype(F32), axis=1, keepdims=True),
                )
            )
    for alive, target, part, lanes in parts:
        at = rows_at(jnp.where(alive, place[target], 0), tile)
        scale = jnp.where(alive, 1.0, 0.0).astype(F32)
        raw[at, :] += part * scale
        deg[at, :] += lanes * scale
    for start in range(0, first, group):
        here = pl.ds(start * tile, group * tile)
        there = [rows_at(order[i], tile) for i in range(start, start + group)]
        o, g, a = dense(
            raw[here, :],
            deg[here, :],
            jnp.concatenate([own[at, :] for at in there]),
            jnp.concatenate([cot[at, :] for at in there]),
            w_neigh,
        )
        out[here, :] = o
        grad[here, :] = g
        agg_grad[here, :] = a
        turned[:, here] = a.T
    for d in range(peers):
        p = col ^ d
        for k in range(slots):
            alive = k < count[0, p]
            at = rows_at(jnp.where(alive, place[dst[k, p]], 0), tile)
            part = lax.dot_general(adj[p, k], agg_grad[at, :], BY_FIRST, preferred_element_type=F32)
            back[d][k] = (part * jnp.where(alive, 1.0, 0.0).astype(F32)).astype(BF16)


def hub_backward_kernel(order, hub_ids, adj, turned, *rest, tile):
    before, (even, odd, acc) = rest[:-3], rest[-3:]
    row = lax.axis_index("row")
    sections = adj.shape[0]
    there = [rows_at(order[i], tile) for i in range(turned.shape[1] // tile)]
    acc[...] = before[0][...] if before else jnp.zeros_like(acc)
    for s in range(sections):
        weights = jnp.concatenate([adj[s, at, :] for at in there])
        acc[hub_ids[s] ^ row] += jnp.dot(turned[...], weights, preferred_element_type=F32)
    for e in range(even.shape[0]):
        even[e] = acc[2 * e].astype(BF16)
        odd[e] = acc[2 * e + 1].astype(BF16)


def self_kernel(order, w_self, *rest, tile):
    pieces, (out, total, self_grad, narrow, sems) = rest[:-5], rest[-5:]
    copies = []
    i = 0
    for outs, grads in zip(pieces[: len(pieces) // 2], pieces[len(pieces) // 2 :]):
        for j in range(outs.shape[0] // tile):
            copies.append(
                pltpu.make_async_copy(outs.at[pl.ds(j * tile, tile)], out.at[rows_at(order[i], tile)], sems.at[i])
            )
            copies[-1].start()
            i += 1
    i = 0
    for grads in pieces[len(pieces) // 2 :]:
        through = lax.dot_general(grads[...], w_self[...], BY_LAST, preferred_element_type=F32)
        for j in range(grads.shape[0] // tile):
            at = rows_at(order[i], tile)
            self_grad[at, :] = through[j * tile : (j + 1) * tile]
            narrow[at, :] = through[j * tile : (j + 1) * tile].astype(BF16)
            i += 1
    parts = sems.shape[0] - len(copies)
    rows = narrow.shape[0] // parts
    for i in range(parts):
        at = pl.ds(i * rows, rows)
        copies.append(pltpu.make_async_copy(narrow.at[at], total.at[at], sems.at[len(copies)]))
        copies[-1].start()
    for copy in copies:
        copy.wait()


def pair_add_kernel(even, came, *outs):
    for e, out in enumerate(outs):
        out[...] = (even[e].astype(F32) + came[e].astype(F32)).astype(BF16)


def final_kernel(send, self_grad, *rest, peers, slots, tile):
    back, hub, (_, out, total, done, sems) = rest[:peers], rest[peers:-5], rest[-5:]
    col = lax.axis_index("col")
    head = pl.ds(0, hub[0].shape[1])
    targets = [send[k, col ^ d] for d in range(peers) for k in range(slots)]
    spots = [rows_at(target, tile) for target in targets]
    total[head, :] = self_grad[head, :]
    for at in spots:
        total[at, :] = self_grad[at, :]
    for i, at in enumerate(spots):
        total[at, :] += back[i // slots][i % slots].astype(F32)
    come = hub[0][...].astype(F32)
    for h in hub[1:]:
        come = come + h[...].astype(F32)
    total[head, :] += come.T
    done[head, :] = total[head, :].astype(BF16)
    copies = [(None, pltpu.make_async_copy(done.at[head], out.at[head], sems.at[len(spots)]))]
    copies[0][1].start()
    for i, at in enumerate(spots):
        fresh = targets[i] * tile >= hub[0].shape[1]
        for other in targets[:i]:
            fresh = fresh & (other != targets[i])
        copy = pltpu.make_async_copy(done.at[at], out.at[at], sems.at[i])
        copies.append((fresh, copy))

        @pl.when(fresh)
        def _(at=at, copy=copy):
            done[at, :] = total[at, :].astype(BF16)
            copy.start()

    for fresh, copy in copies:
        if fresh is None:
            copy.wait()
        else:
            pl.when(fresh)(copy.wait)


def shards(
    features, w_self, w_neigh, bias, hub_ids, hub_adj, send_tile, recv_count, recv_dst, recv_adj, cotangent, *, n_row, n_col
):
    nodes, width = features.shape
    sections, hub_rows = hub_ids.shape[0], hub_adj.shape[3]
    peers, slots, tile = recv_adj.shape[1], recv_adj.shape[2], recv_adj.shape[3]
    out_width = w_self.shape[1]
    tiles = nodes // tile
    first = min(peers * slots, tiles)
    group = 4
    send, count, dst = send_tile.swapaxes(1, 2)[0], recv_count, recv_dst.swapaxes(1, 2)[0]
    adj, weights, bias = hub_adj[0], recv_adj[0], bias.reshape(1, -1)
    params = pltpu.CompilerParams(vmem_limit_bytes=24 * 1024 * 1024)
    shape = jax.ShapeDtypeStruct
    sizes = dict(peers=peers, slots=slots, tile=tile)

    def cost(flops):
        return pl.CostEstimate(flops=flops, transcendentals=0, bytes_accessed=8 * nodes * width)

    def across(x, axis, size, d):
        return lax.ppermute(x, axis, [(i, i ^ d) for i in range(size)])

    order = exchange_order(n_col)
    pair = shape((slots, tile, width), BF16)
    feats, own_hub, *picked = pl.pallas_call(
        pick_kernel,
        in_specs=[HBM, HBM],
        out_specs=[VMEM] * (peers + 2),
        scratch_shapes=[pltpu.SMEM(send.shape, jnp.int32), pltpu.SemaphoreType.DMA((5,))],
        out_shape=[shape((nodes, width), BF16), shape((hub_rows, width), BF16)] + [pair] * peers,
        compiler_params=params,
        cost_estimate=pl.CostEstimate(flops=1000000000, transcendentals=0, bytes_accessed=0),
        name="pick",
    )(pltpu.with_memory_space_constraint(send, pltpu.HBM), pltpu.with_memory_space_constraint(features, pltpu.HBM))
    incoming = [picked[0]] + [None] * (peers - 1)
    for d in order:
        incoming[d] = across(picked[d], "col", n_col, d)
    same = jnp.stack([own_hub] + [across(own_hub, "row", n_row, d) for d in range(2, n_row, 2)])
    other = across(same, "row", n_row, 1)

    own = pl.pallas_call(
        early_kernel,
        in_specs=[VMEM] * 3,
        out_specs=VMEM,
        out_shape=shape((nodes, out_width), F32),
        compiler_params=params,
        cost_estimate=pl.CostEstimate(flops=1000000000, transcendentals=0, bytes_accessed=0),
        name="early",
    )(feats, w_self, bias)
    tile_at, place = pl.pallas_call(
        functools.partial(tile_order, peers=peers, slots=slots, tiles=tiles),
        in_specs=[SMEM] * 2,
        out_specs=[SMEM] * 2,
        out_shape=[shape((tiles,), jnp.int32)] * 2,
        compiler_params=params,
        cost_estimate=pl.CostEstimate(flops=10000000000, transcendentals=0, bytes_accessed=0),
        name="tables",
    )(count, dst)

    def results(number):
        if not number:
            return []
        return [shape((number * tile, out_width), BF16)] * 2 + [shape((width, number * tile), BF16)]

    deg = pl.pallas_call(
        functools.partial(degree_kernel, chunk=256),
        in_specs=[VMEM],
        out_specs=VMEM,
        out_shape=shape((nodes, 128), F32),
        compiler_params=params,
        name="degree",
    )(adj)
    early_shapes = results(tiles - first)[:2]
    if early_shapes:
        early_shapes.append(shape((n_row, width, hub_rows), F32))
    raw, *others = pl.pallas_call(
        functools.partial(forward_kernel, tile=tile, chunk=256, group=group),
        in_specs=[SMEM] * 2 + [VMEM] * 7,
        out_specs=[VMEM] * (1 + len(early_shapes)),
        scratch_shapes=[pltpu.VMEM((sections * hub_rows, width), BF16)]
        + [pltpu.VMEM(x.shape, x.dtype) for x in results(tiles - first)[2:]],
        out_shape=[shape((nodes, width), F32)] + early_shapes,
        compiler_params=params,
        cost_estimate=cost(2 * sections * nodes * hub_rows * width),
        name="forward",
    )(tile_at, hub_ids, adj, same, other, deg, own, cotangent, w_neigh)
    landed = pl.pallas_call(
        functools.partial(landed_kernel, group=group, **sizes),
        in_specs=[SMEM] * 4 + [VMEM] * (6 + peers),
        out_specs=[VMEM] * (3 + peers),
        scratch_shapes=[pltpu.VMEM((first * tile, n), t) for n, t in ((width, F32), (128, F32), (width, BF16))],
        out_shape=results(first) + [pair] * peers,
        compiler_params=params,
        name="landed",
    )(count, dst, tile_at, place, raw, deg, own, cotangent, weights, w_neigh, *incoming)
    outs, grads = zip(*([landed[:2]] + ([others[:2]] if others else [])))
    going = landed[3:]
    returned = [going[0]] + [None] * (peers - 1)
    for d in order:
        returned[d] = across(going[d], "col", n_col, d)

    half = shape((n_row // 2, width, hub_rows), BF16)
    even, odd = pl.pallas_call(
        functools.partial(hub_backward_kernel, tile=tile),
        in_specs=[SMEM] * 2 + [VMEM] * (2 + len(others[2:])),
        out_specs=[VMEM] * 2,
        scratch_shapes=[pltpu.VMEM((n_row, width, hub_rows), F32)],
        out_shape=[half, half],
        compiler_params=params,
        cost_estimate=cost(2 * sections * nodes * hub_rows * width),
        name="hub_backward",
    )(tile_at, hub_ids, adj, landed[2], *others[2:])
    came = across(odd, "row", n_row, 1)
    output, feature_grad, self_grad = pl.pallas_call(
        functools.partial(self_kernel, tile=tile),
        in_specs=[SMEM] + [VMEM] * (1 + 2 * len(outs)),
        out_specs=[HBM, HBM, VMEM],
        scratch_shapes=[pltpu.VMEM((nodes, width), BF16), pltpu.SemaphoreType.DMA((tiles + 4,))],
        out_shape=[shape((nodes, out_width), BF16), shape((nodes, width), BF16), shape((nodes, width), F32)],
        compiler_params=params,
        name="self",
    )(tile_at, w_self, *outs, *grads)
    block = shape((width, hub_rows), BF16)
    sums = pl.pallas_call(
        pair_add_kernel,
        out_shape=[block] * (n_row // 2),
        compiler_params=params,
        name="pair_add",
    )(even, came)
    hubs = [sums[0]] + [across(sums[d // 2], "row", n_row, d) for d in range(2, n_row, 2)]

    feature_grad = pl.pallas_call(
        functools.partial(final_kernel, **sizes),
        in_specs=[SMEM] + [VMEM] * (1 + peers + len(hubs)) + [HBM],
        out_specs=HBM,
        scratch_shapes=[
            pltpu.VMEM((nodes, width), F32),
            pltpu.VMEM((nodes, width), BF16),
            pltpu.SemaphoreType.DMA((peers * slots + 1,)),
        ],
        out_shape=shape((nodes, width), BF16),
        input_output_aliases={2 + peers + len(hubs): 0},
        compiler_params=params,
        name="final",
    )(send, self_grad, *returned, *hubs, feature_grad)
    return (output, feature_grad)


def exchange_order(n_col):
    return sorted(range(1, n_col), key=lambda d: (d != n_col // 2, d))


def solution(mesh):
    blocks = ("row", "col")
    placed = (
        P(blocks, None),
        P(),
        P(),
        P(),
        P(),
        P(blocks, None, None, None),
        P(blocks, None, None),
        P(blocks, None),
        P(blocks, None, None),
        P(blocks, None, None, None, None),
        P(blocks, None),
    )
    n_row, n_col = mesh.shape["row"], mesh.shape["col"]

    def body(*args):
        return shards(*args, n_row=n_row, n_col=n_col)

    return jax.shard_map(
        body, mesh=mesh, in_specs=placed, out_specs=(P(blocks, None), P(blocks, None)), check_vma=False
    )
```
